1024 devices in a mesh: lon: 16 (over x, z_hi), lat: 16 (over z_lo, core), dp: 4 (over y).
Axes of the slice: x: 4, y: 4, z: 32 (z_hi: 4, z_lo: 8; z = z_hi * 8 + z_lo), core: 2. Of those that a mesh axis runs over, the one named last changes fastest.
Arguments:
- tokens: bfloat16 [4, 2, 128, 256, 1024], P('dp', None, 'lat', 'lon'), may hold values from -6 to 6
- norm_gain: float32 [1024], replicated, may hold values from 0.1 to 1.9
- w_qkv: bfloat16 [1024, 3072], replicated, may hold values from -8 to 8
- w_out: bfloat16 [1024, 1024], replicated, may hold values from -0.1875 to 0.1875
- obs_vectors: bfloat16 [65536, 1024], P(('lon', 'lat', 'dp')), may hold values from -6 to 6
- obs_lat: int32 [65536, 1], P(('lon', 'lat', 'dp')), may hold values from 0 to 15; in each aligned block of 64 rows (0 to 63, 64 to 127, ...) at most 6 rows name the same one
- obs_cell: int32 [65536], P(('lon', 'lat', 'dp')), may hold values from 0 to 255
- obs_count: int32 [1024], P(('lon', 'lat', 'dp')), may hold values from 1 to 64, 49152 in all
- shift_offsets: int32 [4, 2], P('dp'), may hold values from 1 to 7, as said below
- cotangent: bfloat16 [4, 2, 128, 256, 1024], P('dp', None, 'lat', 'lon'), may hold values from -0.015625 to 0.015625
Outputs:
- block_out: bfloat16 [4, 2, 128, 256, 1024], P('dp', None, 'lat', 'lon')
- gradient: float32 [1024, 1024], P('lon', ('lat', 'dp'))
The draws below stay inside these ranges and needn't reach their ends.
Inputs may be any that keep to these rules, and one draw needn't show every extreme that they name: `obs_lat`: among the 64 rows of one device at most 6 name the same latitude index; some device has exactly 6 for some index. `obs_count`: some device has exactly 64 live rows. `shift_offsets`: each column takes the value 8 - 1 for some sample.
All inputs are finite; a program needn't handle non-finite values.
Results may differ from the reference program's by a relative error of at most 0.0086.
Values may be sent and summed in bfloat16 or wider, within the bound.
A program may use at most 64 MiB of HBM per device.

```python
import math
import jax
import jax.numpy as jnp
import numpy as np
from jax import lax

D = 1024
HEADS = 16
WIN = 8
LEVELS = 2
LAT_DEV = 8
LON_DEV = 16
OBS_DEV = 64
BATCH = 4
LAT = 128
LON = 256
TOK_DEV = 256
ALL_TOK = 262144
OBS = 65536
CAP = 6
N_LAT = 16
N_DP = 4
DEVICES = 1024


def draw_w_qkv(key, part):
    keys = jax.random.split(key, 1)
    base = jnp.clip(jax.random.normal(keys[0], (D, 3 * D), jnp.float32), -6.0, 6.0) * D ** (-0.5)
    return jnp.clip(base, -8.0, 8.0).astype(jnp.bfloat16)


def draw_shift_offsets(key, part):
    values = jax.random.randint(key, (BATCH, 2), 1, WIN, dtype=jnp.int32)
    chosen = jax.random.randint(jax.random.fold_in(key, 7), (2,), 0, BATCH, dtype=jnp.int32)
    sample_ids = jnp.arange(BATCH, dtype=jnp.int32)
    return jnp.where(sample_ids[:, None] == chosen[None, :], WIN - 1, values).astype(jnp.int32)


def touch_ends(values, rng, least, largest):
    index_at = [jax.random.randint(jax.random.fold_in(rng, axis), (), 0, length) for axis, length in enumerate(values.shape)]
    widest = values.shape.index(max(values.shape))
    next_to = index_at[:widest] + [(index_at[widest] + 1) % values.shape[widest]] + index_at[widest + 1:]
    return values.at[tuple(index_at)].set(least).at[tuple(next_to)].set(largest)


def raised(array, key, source, target, shards_of, factor):
    def block_of(dim):
        return (jnp.arange(array.shape[dim]) // (array.shape[dim] // shards_of)).reshape((-1,) + (1,) * (array.ndim - 1 - dim))

    near = jax.random.permutation(key, shards_of)[block_of(target)]
    second = (block_of(target) + shards_of // 2) % shards_of
    return jnp.where((block_of(source) == near) | (block_of(source) == second), factor * array, array)


def shard_levels(key, shape, cuts, low, largest):
    factor_of, own = 1.0, jax.random.fold_in(key, 6)
    for axis_at, blocks in cuts:
        steps = jnp.exp(jax.random.uniform(jax.random.fold_in(own, axis_at), (blocks,), jnp.float32, low / len(cuts), largest / len(cuts)))
        factor_of = factor_of * jnp.repeat(steps, shape[axis_at] // blocks).reshape([-1 if axis == axis_at else 1 for axis in range(len(shape))])
    return factor_of


def split_up(number_of, total, bound, slope):
    loads = [(1 << 20) // math.isqrt(standing ** slope) + 1 for standing in range(2, number_of + 1)]
    rest, given = total - bound - (number_of - 1), [1] * (number_of - 1)
    while rest > 0:
        free = [i for i in range(number_of - 1) if given[i] < bound]
        whole, remaining = sum([loads[i] for i in free]), rest
        for i in free:
            extra = min(bound - given[i], max(1, remaining * loads[i] // whole), rest)
            given[i] = given[i] + extra
            rest = rest - extra
    return np.array([bound] + given)


def uneven_parts(key, number_of, total, bound, slope):
    if number_of == 2:
        one = jax.random.randint(key, (), max(1, total - bound), min(bound, total - 1) + 1)
        return jnp.stack([one, total - one])
    tallies = jnp.asarray(split_up(number_of, total, bound, slope), jnp.int32)
    couples = (number_of - 1) // 2
    giver, receiver = tallies[1:1 + 2 * couples:2], tallies[2:2 + 2 * couples:2]
    slack = jnp.minimum(giver - 1, bound - receiver)
    moved = jax.random.randint(jax.random.fold_in(key, 1), (couples,), 0, 1 << 20) % (slack + 1)
    tallies = tallies.at[1:1 + 2 * couples:2].set(giver - moved).at[2:2 + 2 * couples:2].set(receiver + moved)
    return tallies[jax.random.permutation(jax.random.fold_in(key, 2), number_of)]


def routed_block(rng, own, number, rows, amount, top, reach, lean):
    sequence = jax.random.permutation(rng, amount)
    packed, common = portions_of(amount, rows * top, reach, lean, True), portions_of(amount, rows * top, reach, lean, False)
    places = jnp.arange(amount)

    def named(sizes, offset_by):
        used = int((sizes > 0).sum())
        fixed = max(1, used // 4)
        shifted = fixed + (places - fixed + offset_by * (used - fixed)) % max(1, amount - fixed)
        return jnp.zeros((amount,), jnp.int32).at[sequence[jnp.where(places < fixed, places, shifted)]].set(jnp.asarray(sizes, jnp.int32))

    sizes = jnp.where(number % 4 == 0, named(packed, number // 4), named(common, number - number // 4 - 1))
    mixed = jax.random.permutation(jax.random.fold_in(own, 3), amount)
    donor, sink = mixed[0:amount // 2 * 2:2], mixed[1:amount // 2 * 2:2]
    slack = jnp.minimum(sizes[donor] - 1, reach - sizes[sink]) // 2
    slack = jnp.where((donor == sequence[0]) | (sink == sequence[0]) | (sizes[sink] == 0), 0, jnp.maximum(slack, 0))
    shifted = jax.random.randint(jax.random.fold_in(own, 4), (amount // 2,), 0, 1 << 20) % (slack + 1)
    sizes = sizes.at[donor].add(-shifted).at[sink].add(shifted)
    labels = jnp.searchsorted(jnp.cumsum(sizes), jnp.arange(rows * top), side="right").astype(jnp.int32)
    grid = labels.reshape(top, rows).T
    grid = grid[jax.random.permutation(jax.random.fold_in(own, 1), rows)]
    offset_by = jax.random.randint(jax.random.fold_in(own, 2), (rows, 1), 0, top)
    return jnp.take_along_axis(grid, (jnp.arange(top)[None, :] + offset_by) % top, axis=1)


def portions_of(amount, total, most, skew, full):
    portions = [(1 << 20) // math.isqrt(grade ** skew) + 1 for grade in range(1, amount + 1)]
    largest = most if full else min(most, max(-(-total // amount), total * portions[0] // sum(portions)))
    least = 1 if total - largest >= amount - 1 else 0
    given, spare = [largest] + [least] * (amount - 1), total - largest - least * (amount - 1)
    while spare > 0:
        free = [i for i in range(1, amount) if given[i] < largest] or [i for i in range(1, amount) if given[i] < most]
        pool, budget = sum([portions[i] for i in free]), spare
        for i in free:
            extra = min(most - given[i], max(1, budget * portions[i] // pool), spare)
            given[i] = given[i] + extra
            spare = spare - extra
    return np.array(given)


def gaussian(key, extent, deviation, bound, shards=(), kind=jnp.bfloat16):
    entries = jax.random.normal(key, extent, jnp.float32) * deviation
    if len(shards) > 0:
        entries = shard_levels(key, extent, shards, -0.22, 0.18) * entries
    return jnp.clip(entries, min=-bound, max=bound).astype(kind)


def gaussian_with(key, extent, scale, limit, shards, heavy, held_as=jnp.bfloat16):
    array = scale * jax.random.normal(key, extent, jnp.float32)
    if shards:
        array = array * shard_levels(key, extent, shards, -0.22, 0.18)
    return jnp.clip(raised(array, jax.random.fold_in(key, 3), *heavy), -limit, limit).astype(held_as)


def setup_inputs(seed: int = 0) -> dict:
    streams_of = jax.random.split(jax.random.key(seed), 11)
    tokens = gaussian(streams_of[0], (BATCH, LEVELS, LAT, LON, D), 1.0, 6.0, ((0, 4), (2, 16), (3, 16)))
    norm_gain = jnp.clip(1.0 + 0.18 * jax.random.normal(streams_of[1], (D,), jnp.float32), 0.1, 1.9)
    w_qkv = draw_w_qkv(jax.random.fold_in(streams_of[10], 71), 0)
    w_out = gaussian(streams_of[3], (D, D), D ** -0.5, 0.1875)
    obs_vectors = gaussian(streams_of[4], (OBS, D), 1.0, 6.0, ((0, 1024),))
    obs_lat_keys = jax.random.split(jax.random.fold_in(streams_of[5], 1), OBS // OBS_DEV)
    obs_lat_turns = jax.random.permutation(jax.random.fold_in(streams_of[5], 3), OBS // OBS_DEV)
    obs_lat = jax.vmap(lambda own, number: routed_block(jax.random.fold_in(streams_of[5], 2), own, number, OBS_DEV, N_LAT, 1, CAP, 2))(obs_lat_keys, obs_lat_turns).reshape((OBS, 1))
    obs_cell = touch_ends(jax.random.randint(streams_of[6], (OBS,), 0, TOK_DEV), jax.random.fold_in(streams_of[6], 1), 0, TOK_DEV - 1).astype(jnp.int32)
    obs_count = uneven_parts(streams_of[7], DEVICES, DEVICES * OBS_DEV * 3 // 4, OBS_DEV, 2).astype(jnp.int32)
    shift_offsets = draw_shift_offsets(jax.random.fold_in(streams_of[10], 71), 0)
    cotangent = gaussian_with(streams_of[9], (BATCH, LEVELS, LAT, LON, D), ALL_TOK ** -0.5, 0.015625, ((0, 4), (2, 16), (3, 16)), (3, 4, 16, 2.0))
    return {"tokens": tokens, "norm_gain": norm_gain, "w_qkv": w_qkv, "w_out": w_out, "obs_vectors": obs_vectors, "obs_lat": obs_lat, "obs_cell": obs_cell, "obs_count": obs_count, "shift_offsets": shift_offsets, "cotangent": cotangent}


def to_windows(field_in):
    levels_n, rows_n, cols_n, feat_width = field_in.shape
    blocks = field_in.reshape(levels_n, rows_n // WIN, WIN, cols_n // WIN, WIN, feat_width)
    return blocks.transpose(1, 3, 0, 2, 4, 5).reshape(-1, levels_n * WIN * WIN, feat_width)

def from_windows(windows, levels_n, rows_n, cols_n):
    feat_width = windows.shape[-1]
    blocks = windows.reshape(rows_n // WIN, cols_n // WIN, levels_n, WIN, WIN, feat_width)
    return blocks.transpose(2, 0, 3, 1, 4, 5).reshape(levels_n, rows_n, cols_n, feat_width)

def window_block(win_tokens, win_valid, norm_gain, w_qkv, w_out):
    n_win, n_tok, d_model = win_tokens.shape
    head_dim = d_model // HEADS
    as_float = win_tokens.astype(jnp.float32)
    average = lax.optimization_barrier(jnp.mean(as_float, axis=-1, keepdims=True))
    centred = as_float - average
    variance = lax.optimization_barrier(jnp.mean(centred * centred, axis=-1, keepdims=True))
    normed = (centred * lax.rsqrt(variance + 1e-05) * norm_gain).astype(jnp.bfloat16)
    projected = jnp.dot(normed.reshape(-1, d_model), w_qkv, preferred_element_type=jnp.float32).astype(jnp.bfloat16)
    projected = projected.reshape(n_win, n_tok, 3, HEADS, head_dim)
    queries = projected[:, :, 0].astype(jnp.float32)
    key_rows = projected[:, :, 1].astype(jnp.float32)
    values = projected[:, :, 2].astype(jnp.float32)
    scores = jnp.einsum('wqhd,wkhd->whqk', queries, key_rows) * head_dim ** (-0.5)
    scores = jnp.where(win_valid[:, None, None, :], scores, -1e+30)
    highest = lax.optimization_barrier(jnp.max(scores, axis=-1, keepdims=True))
    powers = jnp.exp(scores - highest)
    weights = (powers / lax.optimization_barrier(jnp.sum(powers, axis=-1, keepdims=True))).astype(jnp.bfloat16)
    context = jnp.einsum('whqk,wkhd->wqhd', weights.astype(jnp.float32), values).astype(jnp.bfloat16)
    context = context.reshape(n_win, n_tok, d_model)
    result = jnp.dot(context.reshape(-1, d_model), w_out, preferred_element_type=jnp.float32)
    return ((as_float + result.reshape(n_win, n_tok, d_model)).astype(jnp.bfloat16), context)

def reference(tokens, norm_gain, w_qkv, w_out, obs_vectors, obs_lat, obs_cell, obs_count, shift_offsets, cotangent):
    n_batch, levels, n_rows, n_cols, d_model = tokens.shape
    row_ids = jnp.arange(obs_vectors.shape[0], dtype=jnp.int32)
    device = row_ids // OBS_DEV
    within = row_ids % OBS_DEV
    is_live = within < obs_count[device]
    lon_index = device // (N_LAT * N_DP)
    sample = device % N_DP
    level_of = obs_cell // (LAT_DEV * LON_DEV)
    row_of = obs_lat[:, 0] * LAT_DEV + obs_cell // LON_DEV % LAT_DEV
    col_of = lon_index * LON_DEV + obs_cell % LON_DEV
    addend = jnp.where(is_live[:, None], obs_vectors.astype(jnp.float32), jnp.zeros((), jnp.float32))
    enriched = tokens.astype(jnp.float32).at[sample, level_of, row_of, col_of].add(addend).astype(jnp.bfloat16)
    lat_blocks = n_rows // WIN

    def roll_sample(pair):
        grid_in, offset_pair = pair
        turned = jnp.roll(grid_in, -offset_pair[1], axis=2)
        padded = jnp.concatenate([turned, jnp.zeros((levels, WIN, n_cols, d_model), turned.dtype)], axis=1)
        anchor = jnp.zeros((), jnp.int32)
        return lax.dynamic_slice(padded, (anchor, offset_pair[0].astype(jnp.int32), anchor, anchor), grid_in.shape)
    rolled = lax.map(roll_sample, (enriched, shift_offsets))

    def advance(gradient, position):
        sample_at = position // lat_blocks
        start_row = (position % lat_blocks * WIN).astype(jnp.int32)
        strip_in = lax.dynamic_slice_in_dim(rolled[sample_at], start_row, WIN, 1)
        cot_strip = lax.dynamic_slice_in_dim(cotangent[sample_at], start_row, WIN, 1)
        global_rows = start_row + jnp.arange(WIN, dtype=jnp.int32) + shift_offsets[sample_at, 0]
        is_valid = jnp.broadcast_to((global_rows < n_rows)[None, :, None, None], (levels, WIN, n_cols, 1))
        mixed, context = window_block(to_windows(strip_in), to_windows(is_valid)[..., 0], norm_gain, w_qkv, w_out)
        cot_rows = to_windows(cot_strip).reshape(-1, d_model)
        gradient = gradient + jnp.dot(cot_rows.T, context.reshape(-1, d_model), preferred_element_type=jnp.float32)
        return (gradient, from_windows(mixed, levels, WIN, n_cols))
    gradient, strips = lax.scan(advance, jnp.zeros((d_model, d_model), jnp.float32), jnp.arange(n_batch * lat_blocks, dtype=jnp.int32))
    block_out = strips.reshape(n_batch, lat_blocks, levels, WIN, n_cols, d_model).transpose(0, 2, 1, 3, 4, 5).reshape(tokens.shape)
    return (block_out, gradient)
```

```python
import functools

import jax
import jax.numpy as jnp
from jax import lax
from jax.experimental import pallas as pl
from jax.experimental.pallas import tpu as pltpu
from jax.sharding import PartitionSpec as P

HEADS = 16
WIN = 8
MESH = pl.DeviceIdType.MESH


def shifted(array, axis, by):
    devices = lax.axis_size(axis)
    return lax.ppermute(array, axis, [(i, (i + by) % devices) for i in range(devices)])


def from_behind(array, axis, by):
    devices = lax.axis_size(axis)
    pairs = [(i, i + by) for i in range(devices) if 0 <= i + by < devices]
    return lax.ppermute(array, axis, pairs)


def block_kernel(
    base_ref, region_ref, gain_ref, w_qkv_ref, w_out_ref, cot_ref, out_ref, g_ref, qkv_ref, ctx_ref, ctx_t_ref
):
    n_tok, d_model = region_ref.shape
    head_dim = d_model // HEADS
    pair = 2 * head_dim
    groups = n_tok // (2 * WIN)
    win_tok = n_tok // 2
    as_float = region_ref[...].astype(jnp.float32)
    average = jnp.mean(as_float, axis=-1, keepdims=True)
    centred = as_float - average
    variance = jnp.mean(centred * centred, axis=-1, keepdims=True)
    normed = (centred * lax.rsqrt(variance + 1e-05) * gain_ref[...]).astype(jnp.bfloat16)
    block = 512
    for col in range(0, 3 * d_model, block):
        part = jnp.dot(normed, w_qkv_ref[:, col : col + block], preferred_element_type=jnp.float32)
        part = part.reshape(groups, 2, WIN, block)
        for win in range(2):
            qkv_ref[win, :, col : col + block] = part[:, win].reshape(win_tok, block).astype(jnp.bfloat16)
    lane = lax.broadcasted_iota(jnp.int32, (win_tok, pair), 1)
    first = lane < head_dim
    key = lax.broadcasted_iota(jnp.int32, (win_tok, 2 * win_tok), 1)
    is_valid = base_ref[0] + (key // WIN) % WIN < base_ref[1]
    for win in range(2):
        for two in range(HEADS // 2):
            at = two * pair
            queries = qkv_ref[win, :, at : at + pair]
            keys = qkv_ref[win, :, d_model + at : d_model + at + pair]
            values = qkv_ref[win, :, 2 * d_model + at : 2 * d_model + at + pair]
            zero = jnp.zeros_like(keys)
            keys = jnp.concatenate([jnp.where(first, keys, zero), jnp.where(first, zero, keys)], axis=0)
            values = jnp.concatenate([jnp.where(first, values, zero), jnp.where(first, zero, values)], axis=0)
            scores = lax.dot_general(
                queries, keys, (((1,), (1,)), ((), ())), preferred_element_type=jnp.float32
            ) * head_dim ** (-0.5)
            scores = jnp.where(is_valid, scores, -1e30)
            weights = []
            for half in range(2):
                mine = scores[:, half * win_tok : (half + 1) * win_tok]
                powers = jnp.exp(mine - jnp.max(mine, axis=-1, keepdims=True))
                weights.append((powers / jnp.sum(powers, axis=-1, keepdims=True)).astype(jnp.bfloat16))
            context = jnp.dot(jnp.concatenate(weights, axis=1), values, preferred_element_type=jnp.float32)
            ctx_ref[:, win, :, at : at + pair] = context.reshape(groups, WIN, pair)
    context = ctx_ref[...].reshape(n_tok, d_model).astype(jnp.bfloat16)
    for col in range(0, d_model, block):
        result = jnp.dot(context, w_out_ref[:, col : col + block], preferred_element_type=jnp.float32)
        out_ref[:, col : col + block] = (
            region_ref[:, col : col + block].astype(jnp.float32) + result
        ).astype(jnp.bfloat16)
    ctx_t_ref[...] = context.T
    cores, n_x, n_y, rows, wide = g_ref.shape
    n_z = rows // 16
    for x in range(n_x):
        part = jnp.dot(
            ctx_t_ref[...], cot_ref[:, x * wide : (x + 1) * wide], preferred_element_type=jnp.float32
        ).astype(jnp.bfloat16)
        for z in range(n_z):
            for core in range(cores):
                for y in range(n_y):
                    at = ((z * cores + core) * n_y + y) * 16
                    g_ref[core, x, y, z * 16 : (z + 1) * 16, :] = part[at : at + 16, :]


def run_block(base, region, gain, w_qkv, w_out, cot, dims):
    n_tok, d_model = region.shape
    vmem = pl.BlockSpec(memory_space=pltpu.VMEM)
    return pl.pallas_call(
        block_kernel,
        out_shape=(
            jax.ShapeDtypeStruct((n_tok, d_model), jnp.bfloat16),
            jax.ShapeDtypeStruct(dims, jnp.bfloat16),
        ),
        in_specs=[pl.BlockSpec(memory_space=pltpu.SMEM)] + [vmem] * 5,
        out_specs=(vmem, vmem),
        scratch_shapes=[
            pltpu.VMEM((2, n_tok // 2, 3 * d_model), jnp.bfloat16),
            pltpu.VMEM((n_tok // (2 * WIN), 2, WIN, d_model), jnp.float32),
            pltpu.VMEM((d_model, n_tok), jnp.bfloat16),
        ],
        compiler_params=pltpu.CompilerParams(vmem_limit_bytes=40 << 20),
        cost_estimate=pl.CostEstimate(flops=3 << 30, bytes_accessed=12 << 20, transcendentals=1 << 19),
        name="block",
    )(base, region, gain, w_qkv, w_out, cot)


def reduce_kernel(
    n_x, n_y, n_h, n_l,
    g_ref, out_ref,
    c_recv, x_send, x_recv, x_sum, y_send, y_recv, l_send, l_recv, h_send, h_recv,
    c_sems, x_sems, y_sems, l_sems, h_sems,
):
    lon, lat, y = lax.axis_index("lon"), lax.axis_index("lat"), lax.axis_index("dp")
    x, z_hi = lon // n_h, lon % n_h
    z_lo, core = lat // 2, lat % 2
    f32, bf16 = jnp.float32, jnp.bfloat16

    def at_x(k):
        return {"lon": ((x + k) % n_x) * n_h + z_hi}

    def at_y(k):
        return {"dp": (y + k) % n_y}

    def at_l(k):
        return {"lat": ((z_lo + k) % n_l) * 2 + core}

    def at_h(other):
        return {"lon": x * n_h + other}

    pal = {"lat": z_lo * 2 + 1 - core}
    near = z_hi + 1 - 2 * (z_hi % 2)
    far = (z_hi + n_h - 1 + 2 * (z_hi % 2)) % n_h
    peers = [pal] + [at_x(k) for k in range(1, n_x)] + [at_y(k) for k in range(1, n_y)]
    peers += [at_l(k) for k in range(1, n_l)] + [at_h(near), at_h(far)]
    barrier = pltpu.get_barrier_semaphore()
    for peer in peers:
        pl.semaphore_signal(barrier, inc=1, device_id=peer, device_id_type=MESH)
    pl.semaphore_wait(barrier, len(peers))

    def copy(src, dst, sems, k, where):
        return pltpu.make_async_remote_copy(
            src_ref=src, dst_ref=dst, send_sem=sems.at[0, k], recv_sem=sems.at[1, k],
            device_id=where, device_id_type=MESH,
        )

    order = [2, 1, 3, 0] if n_x == 4 else [k for k in range(1, n_x)] + [0]
    c_copies = {}
    for k in order:
        dest = (x + k) % n_x
        c_copies[k] = copy(g_ref.at[1 - core, dest], c_recv.at[k], c_sems, k, pal)
        c_copies[k].start()
    x_copies = {}
    for k in order:
        dest = (x + k) % n_x
        c_copies[k].wait_recv()
        for i in range(n_y):
            part = g_ref[core, dest, i].astype(f32) + c_recv[k, i].astype(f32)
            if k:
                x_send[k - 1, i] = part.astype(bf16)
            else:
                x_sum[i] = part
        if k:
            x_copies[k] = copy(x_send.at[k - 1], x_recv.at[k - 1], x_sems, k - 1, at_x(k))
            x_copies[k].start()
    for k in range(1, n_x):
        x_copies[k].wait_recv()
    y_copies = {}
    for k in list(range(1, n_y)) + [0]:
        dest = (y + k) % n_y
        part = x_sum[dest]
        for j in range(n_x - 1):
            part = part + x_recv[j, dest].astype(f32)
        if k:
            y_send[k - 1] = part.astype(bf16)
            y_copies[k] = copy(y_send.at[k - 1], y_recv.at[k - 1], y_sems, k - 1, at_y(k))
            y_copies[k].start()
    for k in range(1, n_y):
        y_copies[k].wait_recv()
        part = part + y_recv[k - 1].astype(f32)
    rows, wide = part.shape
    l_send[...] = part.reshape(n_l, rows // n_l, wide).astype(bf16)
    x_sum[0] = part
    l_copies = {}
    for k in range(1, n_l):
        l_copies[k] = copy(l_send.at[(z_lo + k) % n_l], l_recv.at[k - 1], l_sems, k - 1, at_l(k))
        l_copies[k].start()
    part = x_sum[0, pl.ds(pl.multiple_of(z_lo * (rows // n_l), rows // n_l), rows // n_l), :]
    for k in range(1, n_l):
        l_copies[k].wait_recv()
        part = part + l_recv[k - 1].astype(f32)
    h_send[0] = part
    first = copy(h_send.at[0], h_recv.at[0], h_sems, 0, at_h(near))
    first.start()
    first.wait_recv()
    part = part + h_recv[0]
    h_send[1] = part
    second = copy(h_send.at[1], h_recv.at[1], h_sems, 1, at_h(far))
    second.start()
    second.wait_recv()
    out_ref[...] = part + h_recv[1]
    for group in (c_copies, x_copies, y_copies, l_copies):
        for k in group:
            group[k].wait_send()
    first.wait_send()
    second.wait_send()


def run_reduce(g, n_h):
    _, n_x, n_y, rows, wide = g.shape
    n_l = rows // 16
    vmem = pl.BlockSpec(memory_space=pltpu.VMEM)
    bf16, f32 = jnp.bfloat16, jnp.float32
    return pl.pallas_call(
        functools.partial(reduce_kernel, n_x, n_y, n_h, n_l),
        out_shape=jax.ShapeDtypeStruct((16, wide), f32),
        in_specs=[vmem],
        out_specs=vmem,
        scratch_shapes=[
            pltpu.VMEM((n_x, n_y, rows, wide), bf16),
            pltpu.VMEM((n_x - 1, n_y, rows, wide), bf16),
            pltpu.VMEM((n_x - 1, n_y, rows, wide), bf16),
            pltpu.VMEM((n_y, rows, wide), f32),
            pltpu.VMEM((n_y - 1, rows, wide), bf16),
            pltpu.VMEM((n_y - 1, rows, wide), bf16),
            pltpu.VMEM((n_l, 16, wide), bf16),
            pltpu.VMEM((n_l - 1, 16, wide), bf16),
            pltpu.VMEM((2, 16, wide), f32),
            pltpu.VMEM((2, 16, wide), f32),
            pltpu.SemaphoreType.DMA((2, n_x)),
            pltpu.SemaphoreType.DMA((2, n_x - 1)),
            pltpu.SemaphoreType.DMA((2, n_y - 1)),
            pltpu.SemaphoreType.DMA((2, n_l - 1)),
            pltpu.SemaphoreType.DMA((2, 2)),
        ],
        compiler_params=pltpu.CompilerParams(
            collective_id=0, has_side_effects=True, vmem_limit_bytes=24 << 20
        ),
        name="reduce",
    )(g)


def on_device(
    tokens,
    norm_gain,
    w_qkv,
    w_out,
    obs_vectors,
    obs_lat,
    obs_cell,
    obs_count,
    shift_offsets,
    cotangent,
):
    n_batch, levels, lat_dev, lon_dev, d_model = tokens.shape
    n_lat = lax.axis_size("lat")
    n_dp = lax.axis_size("dp")
    n_hi = 4
    n_x = lax.axis_size("lon") // n_hi
    obs_rows = obs_vectors.shape[0]
    capacity = obs_rows * 3 // (2 * n_lat)
    n_slots = n_lat * capacity
    destination = obs_lat[:, 0]
    one_hot = (destination[:, None] == jnp.arange(n_lat, dtype=jnp.int32)[None, :]).astype(
        jnp.int32
    )
    earlier = jnp.cumsum(one_hot, axis=0) - one_hot
    rank_in = jnp.sum(earlier * one_hot, axis=1)
    slot_of = destination * capacity + rank_in
    is_live = jnp.arange(obs_rows, dtype=jnp.int32) < obs_count[0]
    cell_tag = jnp.where(is_live, obs_cell, -1)
    chooser = slot_of[None, :] == jnp.arange(n_slots, dtype=jnp.int32)[:, None]
    sent_rows = (
        jnp.dot(chooser.astype(jnp.bfloat16), obs_vectors, preferred_element_type=jnp.float32)
        .astype(jnp.bfloat16)
        .reshape(n_lat, capacity, d_model)
    )
    sent_tags = (jnp.sum(chooser.astype(jnp.int32) * (cell_tag[None, :] + 1), axis=1) - 1).reshape(
        n_lat, capacity
    )
    got_rows, got_tags = (
        lax.all_to_all(sent_rows, "lat", split_axis=0, concat_axis=0, tiled=True),
        lax.all_to_all(sent_tags, "lat", split_axis=0, concat_axis=0, tiled=True),
    )
    flat_tokens = tokens.reshape(-1, d_model)
    placer = (
        got_tags.reshape(-1)[None, :] == jnp.arange(flat_tokens.shape[0], dtype=jnp.int32)[:, None]
    ).astype(jnp.bfloat16)
    added = jnp.dot(placer, got_rows.reshape(-1, d_model), preferred_element_type=jnp.float32)
    enriched = (flat_tokens.astype(jnp.float32) + added).astype(jnp.bfloat16).reshape(tokens.shape)
    margin = WIN - 1
    east_cols = shifted(enriched[:, :, :, :margin], "lon", -1)
    widened = jnp.concatenate([enriched, east_cols], axis=3)
    north_part = from_behind(widened[:, :, :margin], "lat", -1)
    extended = jnp.concatenate([widened, north_part], axis=2)
    lat_shift = shift_offsets[0, 0]
    lon_shift = shift_offsets[0, 1]
    anchor = jnp.zeros((), jnp.int32)
    region = lax.dynamic_slice(
        extended, (anchor, anchor, lat_shift, lon_shift, anchor), tokens.shape
    )[0]
    base = jnp.stack([lax.axis_index("lat") * lat_dev + lat_shift, jnp.int32(lat_dev * n_lat)])
    n_tok = levels * lat_dev * lon_dev
    mixed, partial_sums = run_block(
        base,
        region.reshape(n_tok, d_model),
        norm_gain[None, :],
        w_qkv,
        w_out,
        cotangent.reshape(n_tok, d_model),
        (2, n_x, n_dp, d_model // (2 * n_dp), d_model // n_x),
    )
    reduced = run_reduce(partial_sums, n_hi)
    wide = d_model // (n_x * n_hi)
    start = (lax.axis_index("lon") % n_hi) * wide
    gradient = lax.dynamic_slice(reduced, (anchor, start), (reduced.shape[0], wide)).T
    return (mixed.reshape(tokens.shape), gradient)


def solution(mesh):
    placed = (
        P("dp", None, "lat", "lon", None),
        P(),
        P(),
        P(),
        P(("lon", "lat", "dp"), None),
        P(("lon", "lat", "dp"), None),
        P(("lon", "lat", "dp")),
        P(("lon", "lat", "dp")),
        P("dp", None),
        P("dp", None, "lat", "lon", None),
    )
    return jax.shard_map(
        on_device,
        mesh=mesh,
        in_specs=placed,
        out_specs=(P("dp", None, "lat", "lon", None), P("lon", ("lat", "dp"))),
        check_vma=False,
    )
```

```python
import functools

import jax
import jax.numpy as jnp
from jax import lax
from jax.experimental import pallas as pl
from jax.experimental.pallas import tpu as pltpu
from jax.sharding import PartitionSpec as P

HEADS = 16
WIN = 8
MESH = pl.DeviceIdType.MESH


def exchange_kernel(
    n_x, n_h,
    count_ref, tok_hbm, obs_hbm, lat_hbm, cell_hbm, gain_hbm, w_qkv_hbm, w_out_hbm, cot_hbm,
    own_ref, next_ref, gain_ref, w_qkv_ref, w_out_ref, cot_ref,
    tok_ref, obs_ref, lat_ref, cell_ref, send, recv, l_sems, o_sems, e_sems, n_sems, c_sems,
):
    loads = []
    for src, dst in (
        (lat_hbm, lat_ref), (cell_hbm, cell_ref), (obs_hbm, obs_ref), (tok_hbm, tok_ref),
        (gain_hbm, gain_ref), (cot_hbm, cot_ref), (w_qkv_hbm, w_qkv_ref), (w_out_hbm, w_out_ref),
    ):
        loads.append(pltpu.make_async_copy(src, dst, l_sems.at[len(loads)]))
        loads[-1].start()
    lon, lat = lax.axis_index("lon"), lax.axis_index("lat")
    n_lon = n_x * n_h
    n_lat = send.shape[0]
    f32, bf16, i32 = jnp.float32, jnp.bfloat16, jnp.int32
    west = {"lon": (lon + n_lon - 1) % n_lon}
    east = {"lon": (lon + 1) % n_lon}
    south = {"lat": (lat + n_lat - 1) % n_lat}
    others = [{"lat": (lat + k) % n_lat} for k in range(1, n_lat)]
    barrier = pltpu.get_barrier_semaphore()
    for peer in others + [west, east]:
        pl.semaphore_signal(barrier, inc=1, device_id=peer, device_id_type=MESH)

    for one in loads[:3]:
        one.wait()
    n_obs, d_model = obs_ref.shape
    n_slots = n_lat * 8
    slot = lax.broadcasted_iota(i32, (n_slots, n_obs), 0)
    bound = lat_ref[...] == slot // 8
    earlier = lax.broadcasted_iota(i32, (n_obs, n_obs), 0) < lax.broadcasted_iota(i32, (n_obs, n_obs), 1)
    rank = jnp.dot(bound.astype(f32).astype(bf16), earlier.astype(f32).astype(bf16), preferred_element_type=f32)
    chooser = jnp.where(bound & (rank == (slot % 8).astype(f32)), 1.0, 0.0).astype(bf16)
    rows = jnp.dot(chooser, obs_ref[...], preferred_element_type=f32).reshape(n_lat, 8, d_model)
    live = lax.broadcasted_iota(i32, (8, n_obs), 1) < count_ref[0]
    tags = jnp.where(live, cell_ref[...] + 1, 0).astype(f32).astype(bf16)
    tags = lax.dot_general(tags, chooser, (((1,), (1,)), ((), ())), preferred_element_type=f32)
    at_tag = lax.broadcasted_iota(i32, (n_lat, 8, n_slots), 1) == 6
    send[:, :, :n_slots] = jnp.where(at_tag, tags[None], rows[:, :, :n_slots]).astype(bf16)
    send[:, :, n_slots:] = rows[:, :, n_slots:].astype(bf16)
    recv[lat] = send[lat]

    pl.semaphore_wait(barrier, len(others) + 2)

    def copy(src, dst, sems, k, where):
        return pltpu.make_async_remote_copy(
            src_ref=src, dst_ref=dst, send_sem=sems.at[0, k], recv_sem=sems.at[1, k],
            device_id=where, device_id_type=MESH,
        )

    o_copies = [
        copy(send.at[(lat + k) % n_lat], recv.at[lat], o_sems, k - 1, others[k - 1]) for k in range(1, n_lat)
    ]
    for one in o_copies:
        one.start()
    loads[3].wait()
    n_col, col_rows, _ = own_ref.shape
    lon_dev = tok_ref.shape[0] // col_rows
    margin = n_col - lon_dev
    n_tok = lon_dev * col_rows
    place = lax.broadcasted_iota(i32, (n_tok, n_tok), 0)
    cell = (place % col_rows) * lon_dev + place // col_rows
    mover = jnp.where(cell == lax.broadcasted_iota(i32, (n_tok, n_tok), 1), 1.0, 0.0).astype(bf16)
    turned = jnp.dot(mover, tok_ref[...], preferred_element_type=f32)
    for one in o_copies:
        one.wait_recv()
    got = recv[...].astype(f32)
    slots = got[:, :, :n_slots]
    sub = lax.broadcasted_iota(i32, slots.shape, 1)
    tag = jnp.sum(jnp.where(sub == 6, slots, 0.0), axis=1, keepdims=True)
    lane = lax.broadcasted_iota(i32, slots.shape, 2)
    tag = jnp.sum(jnp.where(lane == lat * 8 + sub, tag, 0.0), axis=2, keepdims=True)
    tag = tag.reshape(n_slots, 1)
    place = lax.broadcasted_iota(i32, (n_slots, n_tok), 1)
    cell = (place % col_rows) * lon_dev + place // col_rows + 1
    placer = jnp.where(tag == cell.astype(f32), 1.0, 0.0).astype(bf16)
    added = lax.dot_general(
        placer, got.reshape(n_slots, d_model).astype(bf16), (((0,), (0,)), ((), ())), preferred_element_type=f32
    )
    own_ref[:lon_dev] = (turned + added).astype(bf16).reshape(lon_dev, col_rows, d_model)

    e_copies = [copy(own_ref.at[j], own_ref.at[lon_dev + j], e_sems, j, west) for j in range(margin)]
    for one in e_copies:
        one.start()
    half = lon_dev // 2
    n_copies = [
        copy(own_ref.at[pl.ds(h * half, half)], next_ref.at[pl.ds(h * half, half)], n_sems, h, south)
        for h in range(2)
    ]
    c_copies = [
        copy(own_ref.at[lon_dev + j], next_ref.at[lon_dev + j], c_sems, j, south) for j in range(margin)
    ]

    @pl.when(lat > 0)
    def _():
        for one in n_copies:
            one.start()

    @pl.when(lat == n_lat - 1)
    def _():
        next_ref[...] = jnp.zeros_like(next_ref)

    for j in range(margin):
        e_copies[j].wait_recv()

        @pl.when(lat > 0)
        def _():
            c_copies[j].start()

    @pl.when(lat < n_lat - 1)
    def _():
        for one in n_copies + c_copies:
            one.wait_recv()

    @pl.when(lat > 0)
    def _():
        for one in n_copies + c_copies:
            one.wait_send()

    for one in o_copies + e_copies:
        one.wait_send()
    for one in loads[4:]:
        one.wait()


def run_exchange(count, arrays, n_lat, n_x, n_h, n_col, col_rows):
    tokens, obs, lats, cells = arrays[:4]
    d_model = obs.shape[1]
    margin = WIN - 1
    vmem = pl.BlockSpec(memory_space=pltpu.VMEM)
    bf16 = jnp.bfloat16
    block = jax.ShapeDtypeStruct((n_col, col_rows, d_model), bf16)
    return pl.pallas_call(
        functools.partial(exchange_kernel, n_x, n_h),
        out_shape=[block, block] + [jax.ShapeDtypeStruct(one.shape, one.dtype) for one in arrays[4:]],
        in_specs=[pl.BlockSpec(memory_space=pltpu.SMEM)] + [pl.BlockSpec(memory_space=pltpu.HBM)] * len(arrays),
        out_specs=[vmem] * (len(arrays) - 2),
        scratch_shapes=[
            pltpu.VMEM(tokens.shape, bf16),
            pltpu.VMEM(obs.shape, bf16),
            pltpu.VMEM(lats.shape, jnp.int32),
            pltpu.VMEM(cells.shape, jnp.int32),
            pltpu.VMEM((n_lat, 8, d_model), bf16),
            pltpu.VMEM((n_lat, 8, d_model), bf16),
            pltpu.SemaphoreType.DMA((len(arrays),)),
            pltpu.SemaphoreType.DMA((2, n_lat - 1)),
            pltpu.SemaphoreType.DMA((2, margin)),
            pltpu.SemaphoreType.DMA((2, 2)),
            pltpu.SemaphoreType.DMA((2, margin)),
        ],
        compiler_params=pltpu.CompilerParams(
            collective_id=1, has_side_effects=True, vmem_limit_bytes=32 << 20
        ),
        cost_estimate=pl.CostEstimate(flops=1 << 28, bytes_accessed=80 << 20, transcendentals=0),
        name="exchange",
    )(count, *[pltpu.with_memory_space_constraint(one, pltpu.HBM) for one in arrays])


def block_kernel(
    lat_dev, shift_ref, own_ref, next_ref, gain_ref, w_qkv_ref, w_out_ref, cot_ref, out_ref, g_ref,
    region_ref, qkv_ref, ctx_ref, ctx_t_ref,
):
    n_tok, d_model = region_ref.shape
    n_src = own_ref.shape[0]
    lon_dev = 2 * WIN
    col_rows = n_tok // lon_dev
    lat_shift, lon_shift = shift_ref[0, 0], shift_ref[0, 1]
    base = lax.axis_index("lat") * lat_dev + lat_shift
    limit = lax.axis_size("lat") * lat_dev
    token = lax.broadcasted_iota(jnp.int32, (n_tok, n_src), 0)
    row = (token // lon_dev) % lat_dev + lat_shift
    source = (token % lon_dev + lon_shift) * col_rows + (token // (lon_dev * lat_dev)) * lat_dev + row
    source = source - lax.broadcasted_iota(jnp.int32, (n_tok, n_src), 1)
    here = jnp.where((source == 0) & (row < lat_dev), 1.0, 0.0).astype(jnp.bfloat16)
    after = jnp.where((source == lat_dev) & (row >= lat_dev), 1.0, 0.0)
    after = jnp.where(row + lax.axis_index("lat") * lat_dev < limit, after, 0.0).astype(jnp.bfloat16)
    region_ref[...] = jnp.dot(here, own_ref[...], preferred_element_type=jnp.float32) + jnp.dot(
        after, next_ref[...], preferred_element_type=jnp.float32
    )
    head_dim = d_model // HEADS
    pair = 2 * head_dim
    groups = n_tok // (2 * WIN)
    win_tok = n_tok // 2
    as_float = region_ref[...]
    average = jnp.mean(as_float, axis=-1, keepdims=True)
    centred = as_float - average
    variance = jnp.mean(centred * centred, axis=-1, keepdims=True)
    normed = (centred * lax.rsqrt(variance + 1e-05) * gain_ref[...]).astype(jnp.bfloat16)
    block = 512
    for col in range(0, 3 * d_model, block):
        part = jnp.dot(normed, w_qkv_ref[:, col : col + block], preferred_element_type=jnp.float32)
        part = part.reshape(groups, 2, WIN, block)
        for win in range(2):
            qkv_ref[win, :, col : col + block] = part[:, win].reshape(win_tok, block).astype(jnp.bfloat16)
    lane = lax.broadcasted_iota(jnp.int32, (win_tok, pair), 1)
    first = lane < head_dim
    key = lax.broadcasted_iota(jnp.int32, (win_tok, 2 * win_tok), 1)
    is_valid = base + (key // WIN) % WIN < limit
    for win in range(2):
        for two in range(HEADS // 2):
            at = two * pair
            queries = qkv_ref[win, :, at : at + pair]
            keys = qkv_ref[win, :, d_model + at : d_model + at + pair]
            values = qkv_ref[win, :, 2 * d_model + at : 2 * d_model + at + pair]
            zero = jnp.zeros_like(keys)
            keys = jnp.concatenate([jnp.where(first, keys, zero), jnp.where(first, zero, keys)], axis=0)
            values = jnp.concatenate([jnp.where(first, values, zero), jnp.where(first, zero, values)], axis=0)
            scores = lax.dot_general(
                queries, keys, (((1,), (1,)), ((), ())), preferred_element_type=jnp.float32
            ) * head_dim ** (-0.5)
            scores = jnp.where(is_valid, scores, -1e30)
            weights = []
            for half in range(2):
                mine = scores[:, half * win_tok : (half + 1) * win_tok]
                powers = jnp.exp(mine - jnp.max(mine, axis=-1, keepdims=True))
                weights.append((powers / jnp.sum(powers, axis=-1, keepdims=True)).astype(jnp.bfloat16))
            context = jnp.dot(jnp.concatenate(weights, axis=1), values, preferred_element_type=jnp.float32)
            ctx_ref[:, win, :, at : at + pair] = context.reshape(groups, WIN, pair)
    context = ctx_ref[...].reshape(n_tok, d_model).astype(jnp.bfloat16)
    for col in range(0, d_model, block):
        result = jnp.dot(context, w_out_ref[:, col : col + block], preferred_element_type=jnp.float32)
        out_ref[:, col : col + block] = (region_ref[:, col : col + block] + result).astype(jnp.bfloat16)
    ctx_t_ref[...] = context.T
    cores, n_x, n_y, rows, wide = g_ref.shape
    n_z = rows // 16
    for x in range(n_x):
        part = jnp.dot(
            ctx_t_ref[...], cot_ref[:, x * wide : (x + 1) * wide], preferred_element_type=jnp.float32
        ).astype(jnp.bfloat16)
        for z in range(n_z):
            for core in range(cores):
                for y in range(n_y):
                    at = ((z * cores + core) * n_y + y) * 16
                    g_ref[core, x, y, z * 16 : (z + 1) * 16, :] = part[at : at + 16, :]


def run_block(lat_dev, shift, own, after, gain, w_qkv, w_out, cot, dims):
    n_tok, d_model = cot.shape
    vmem = pl.BlockSpec(memory_space=pltpu.VMEM)
    return pl.pallas_call(
        functools.partial(block_kernel, lat_dev),
        out_shape=(
            jax.ShapeDtypeStruct((n_tok, d_model), jnp.bfloat16),
            jax.ShapeDtypeStruct(dims, jnp.bfloat16),
        ),
        in_specs=[pl.BlockSpec(memory_space=pltpu.SMEM)] + [vmem] * 6,
        out_specs=(vmem, vmem),
        scratch_shapes=[
            pltpu.VMEM((n_tok, d_model), jnp.float32),
            pltpu.VMEM((2, n_tok // 2, 3 * d_model), jnp.bfloat16),
            pltpu.VMEM((n_tok // (2 * WIN), 2, WIN, d_model), jnp.float32),
            pltpu.VMEM((d_model, n_tok), jnp.bfloat16),
        ],
        compiler_params=pltpu.CompilerParams(vmem_limit_bytes=40 << 20),
        cost_estimate=pl.CostEstimate(flops=3 << 30, bytes_accessed=12 << 20, transcendentals=1 << 19),
        name="block",
    )(shift, own, after, gain, w_qkv, w_out, cot)


def reduce_kernel(
    n_x, n_y, n_h, n_l,
    g_ref, out_ref,
    c_recv_a, c_recv_b, x_send, x_recv, x_sum, y_send, y_recv, y_sum,
    a_send, a_recv, b_send, b_recv, l_send, l_recv, h_send, h_recv, t_send, t_recv,
    c_sems, x_sems, y_sems, a_sems, b_sems, l_sems, h_sems,
):
    lon, lat, y = lax.axis_index("lon"), lax.axis_index("lat"), lax.axis_index("dp")
    x, z_hi = lon // n_h, lon % n_h
    z_lo, core = lat // 2, lat % 2
    f32, bf16 = jnp.float32, jnp.bfloat16

    def at_x(k):
        return {"lon": ((x + k) % n_x) * n_h + z_hi}

    def at_y(k):
        return {"dp": (y + k) % n_y}

    def at_l(k):
        return {"lat": ((z_lo + k) % n_l) * 2 + core}

    def at_h(other):
        return {"lon": x * n_h + other}

    pal = {"lat": z_lo * 2 + 1 - core}
    near = z_hi + 1 - 2 * (z_hi % 2)
    far = (z_hi + n_h - 1 + 2 * (z_hi % 2)) % n_h
    peers = [pal] + [at_x(k) for k in range(1, n_x)] + [at_y(k) for k in range(1, n_y)]
    peers += [at_l(k) for k in range(1, n_l)] + [at_h(near), at_h(far)]
    barrier = pltpu.get_barrier_semaphore()
    for peer in peers:
        pl.semaphore_signal(barrier, inc=1, device_id=peer, device_id_type=MESH)
    pl.semaphore_wait(barrier, len(peers))
    copies = []

    def send(src, dst, sems, k, where):
        one = pltpu.make_async_remote_copy(
            src_ref=src, dst_ref=dst, send_sem=sems.at[0, k], recv_sem=sems.at[1, k],
            device_id=where, device_id_type=MESH,
        )
        one.start()
        copies.append(one)
        return one

    _, _, _, rows, wide = g_ref.shape
    half = rows // 2
    low, high = pl.ds(0, half), pl.ds(half, half)
    order = [2, 1, 3, 0]
    c_a, c_b = {}, {}
    for i, k in enumerate(order):
        dest = (x + k) % n_x
        c_a[k] = send(g_ref.at[1 - core, dest, :, low], c_recv_a.at[k], c_sems, 2 * i, pal)
        dest = (y + k) % n_y
        c_b[k] = send(g_ref.at[1 - core, :, dest, high], c_recv_b.at[k], c_sems, 2 * i + 1, pal)
    x_c, y_c = {}, {}
    for k in order:
        c_a[k].wait_recv()
        dest = (x + k) % n_x
        for i in range(n_y):
            part = g_ref[core, dest, i, :half].astype(f32) + c_recv_a[k, i].astype(f32)
            if k:
                x_send[k - 1, i] = part.astype(bf16)
            else:
                x_sum[i] = part
        if k:
            x_c[k] = send(x_send.at[k - 1], x_recv.at[k - 1], x_sems, k - 1, at_x(k))
        c_b[k].wait_recv()
        dest = (y + k) % n_y
        for i in range(n_x):
            part = g_ref[core, i, dest, half:].astype(f32) + c_recv_b[k, i].astype(f32)
            if k:
                y_send[k - 1, i] = part.astype(bf16)
            else:
                y_sum[i] = part
        if k:
            y_c[k] = send(y_send.at[k - 1], y_recv.at[k - 1], y_sems, k - 1, at_y(k))
    for k in range(1, n_x):
        x_c[k].wait_recv()
    a_c, b_c = {}, {}
    for k in order:
        dest = (y + k) % n_y
        part_a = x_sum[dest]
        for j in range(n_x - 1):
            part_a = part_a + x_recv[j, dest].astype(f32)
        if k:
            a_send[k - 1] = part_a.astype(bf16)
            a_c[k] = send(a_send.at[k - 1], a_recv.at[k - 1], a_sems, k - 1, at_y(k))
    for k in range(1, n_y):
        y_c[k].wait_recv()
    for k in order:
        dest = (x + k) % n_x
        part_b = y_sum[dest]
        for j in range(n_y - 1):
            part_b = part_b + y_recv[j, dest].astype(f32)
        if k:
            b_send[k - 1] = part_b.astype(bf16)
            b_c[k] = send(b_send.at[k - 1], b_recv.at[k - 1], b_sems, k - 1, at_x(k))
    for k in range(1, n_y):
        a_c[k].wait_recv()
        part_a = part_a + a_recv[k - 1].astype(f32)
    for k in range(1, n_x):
        b_c[k].wait_recv()
        part_b = part_b + b_recv[k - 1].astype(f32)
    x_sum[0] = part_a
    x_sum[1] = part_b
    each = rows // n_l
    l_send[: n_l // 2] = part_a.reshape(n_l // 2, each, wide).astype(bf16)
    l_send[n_l // 2 :] = part_b.reshape(n_l // 2, each, wide).astype(bf16)
    l_c = {}
    for k in range(1, n_l):
        l_c[k] = send(l_send.at[(z_lo + k) % n_l], l_recv.at[k - 1], l_sems, k - 1, at_l(k))
    mine = pl.ds(pl.multiple_of((z_lo % (n_l // 2)) * each, each), each)
    part = x_sum[z_lo // (n_l // 2), mine, :]
    for k in range(1, n_l):
        l_c[k].wait_recv()
        part = part + l_recv[k - 1].astype(f32)
    h_send[...] = part.astype(bf16)
    first = send(h_send, h_recv, h_sems, 0, at_h(near))
    first.wait_recv()
    part = part + h_recv[...].astype(f32)
    tile = wide // 2
    left, right = part[:, :tile], part[:, tile:]
    t_send[...] = jnp.where(far // 2 == 0, left, right)
    second = send(t_send, t_recv, h_sems, 1, at_h(far))
    part = jnp.where(z_hi // 2 == 0, left, right)
    second.wait_recv()
    part = part + t_recv[...]
    out_ref[...] = jnp.where(z_hi % 2 == 0, part[:, : tile // 2], part[:, tile // 2 :])
    for one in copies:
        one.wait_send()


def run_reduce(g, n_h):
    _, n_x, n_y, rows, wide = g.shape
    n_l = rows // 16
    half = rows // 2
    vmem = pl.BlockSpec(memory_space=pltpu.VMEM)
    bf16, f32 = jnp.bfloat16, jnp.float32
    sems = pltpu.SemaphoreType.DMA
    return pl.pallas_call(
        functools.partial(reduce_kernel, n_x, n_y, n_h, n_l),
        out_shape=jax.ShapeDtypeStruct((16, wide // n_h), f32),
        in_specs=[vmem],
        out_specs=vmem,
        scratch_shapes=[
            pltpu.VMEM((n_x, n_y, half, wide), bf16),
            pltpu.VMEM((n_y, n_x, half, wide), bf16),
            pltpu.VMEM((n_x - 1, n_y, half, wide), bf16),
            pltpu.VMEM((n_x - 1, n_y, half, wide), bf16),
            pltpu.VMEM((n_y, half, wide), f32),
            pltpu.VMEM((n_y - 1, n_x, half, wide), bf16),
            pltpu.VMEM((n_y - 1, n_x, half, wide), bf16),
            pltpu.VMEM((n_x, half, wide), f32),
            pltpu.VMEM((n_y - 1, half, wide), bf16),
            pltpu.VMEM((n_y - 1, half, wide), bf16),
            pltpu.VMEM((n_x - 1, half, wide), bf16),
            pltpu.VMEM((n_x - 1, half, wide), bf16),
            pltpu.VMEM((n_l, 16, wide), bf16),
            pltpu.VMEM((n_l - 1, 16, wide), bf16),
            pltpu.VMEM((16, wide), bf16),
            pltpu.VMEM((16, wide), bf16),
            pltpu.VMEM((16, wide // 2), f32),
            pltpu.VMEM((16, wide // 2), f32),
            sems((2, 2 * n_x)),
            sems((2, n_x - 1)),
            sems((2, n_y - 1)),
            sems((2, n_y - 1)),
            sems((2, n_x - 1)),
            sems((2, n_l - 1)),
            sems((2, 2)),
        ],
        compiler_params=pltpu.CompilerParams(
            collective_id=0, has_side_effects=True, vmem_limit_bytes=24 << 20
        ),
        name="reduce",
    )(g)


def on_device(
    tokens,
    norm_gain,
    w_qkv,
    w_out,
    obs_vectors,
    obs_lat,
    obs_cell,
    obs_count,
    shift_offsets,
    cotangent,
):
    n_batch, levels, lat_dev, lon_dev, d_model = tokens.shape
    n_lat = lax.axis_size("lat")
    n_dp = lax.axis_size("dp")
    n_hi = 4
    n_x = lax.axis_size("lon") // n_hi
    n_obs = obs_vectors.shape[0]
    n_col = lon_dev + WIN - 1
    arrays = (
        tokens.reshape(-1, d_model),
        obs_vectors,
        obs_lat.reshape(1, n_obs),
        obs_cell[None, :],
        norm_gain[None, :],
        w_qkv,
        w_out,
        cotangent.reshape(-1, d_model),
    )
    own, after, gain, w_qkv, w_out, cot = run_exchange(
        obs_count, arrays, n_lat, n_x, n_hi, n_col, levels * lat_dev
    )
    mixed, partial_sums = run_block(
        lat_dev,
        shift_offsets,
        own.reshape(-1, d_model),
        after.reshape(-1, d_model),
        gain,
        w_qkv,
        w_out,
        cot,
        (2, n_x, n_dp, d_model // (2 * n_dp), d_model // n_x),
    )
    reduced = run_reduce(partial_sums, n_hi)
    gradient = reduced.T
    return (mixed.reshape(tokens.shape), gradient)


def solution(mesh):
    placed = (
        P("dp", None, "lat", "lon", None),
        P(),
        P(),
        P(),
        P(("lon", "lat", "dp"), None),
        P(("lon", "lat", "dp"), None),
        P(("lon", "lat", "dp")),
        P(("lon", "lat", "dp")),
        P("dp", None),
        P("dp", None, "lat", "lon", None),
    )
    return jax.shard_map(
        on_device,
        mesh=mesh,
        in_specs=placed,
        out_specs=(P("dp", None, "lat", "lon", None), P("lon", ("lat", "dp"))),
        check_vma=False,
    )
```

```python
import functools

import jax
import jax.numpy as jnp
from jax import lax
from jax.experimental import pallas as pl
from jax.experimental.pallas import tpu as pltpu
from jax.sharding import PartitionSpec as P

HEADS = 16
WIN = 8
MESH = pl.DeviceIdType.MESH


def exchange_part(
    n_x, n_h, peers,
    count_ref, tok_hbm, obs_hbm, lat_hbm, cell_hbm, gain_hbm, w_qkv_hbm, w_out_hbm, cot_hbm,
    own_ref, next_ref, gain_ref, w_qkv_ref, w_out_ref, cot_ref,
    tok_ref, obs_ref, lat_ref, cell_ref, send, recv, r_one, r_two,
    l_sems, o_sems, e_sems, n_sems, c_sems, r_sems,
):
    loads = []
    for src, dst in (
        (lat_hbm, lat_ref), (cell_hbm, cell_ref), (obs_hbm, obs_ref), (tok_hbm, tok_ref),
        (gain_hbm, gain_ref), (cot_hbm, cot_ref), (w_qkv_hbm, w_qkv_ref), (w_out_hbm, w_out_ref),
    ):
        loads.append(pltpu.make_async_copy(src, dst, l_sems.at[len(loads)]))
        loads[-1].start()
    lon, lat = lax.axis_index("lon"), lax.axis_index("lat")
    n_lon = n_x * n_h
    n_lat = send.shape[0]
    f32, bf16, i32 = jnp.float32, jnp.bfloat16, jnp.int32
    x, z_hi = lon // n_h, lon % n_h
    west = {"lon": (lon + n_lon - 1) % n_lon}
    east = {"lon": (lon + 1) % n_lon}
    south = {"lat": (lat + n_lat - 1) % n_lat}
    others = [{"lat": (lat + k) % n_lat} for k in range(1, n_lat)]
    up = {"lon": x * n_h + (z_hi + 1) % n_h}
    turn = jnp.where(z_hi == n_h - 2, n_x - 1, 0)
    last = {"lon": ((x + turn) % n_x) * n_h + (z_hi + 1) % n_h}
    turn = jnp.where(z_hi == n_h - 1, 1, 0)
    before = {"lon": ((x + turn) % n_x) * n_h + (z_hi + n_h - 1) % n_h}
    barrier = pltpu.get_barrier_semaphore()
    peers = others + [west, east, last, before] + peers
    for peer in peers:
        pl.semaphore_signal(barrier, inc=1, device_id=peer, device_id_type=MESH)

    for one in loads[:3]:
        one.wait()
    n_obs, d_model = obs_ref.shape
    n_slots = n_lat * 8
    slot = lax.broadcasted_iota(i32, (n_slots, n_obs), 0)
    bound = lat_ref[...] == slot // 8
    earlier = lax.broadcasted_iota(i32, (n_obs, n_obs), 0) < lax.broadcasted_iota(i32, (n_obs, n_obs), 1)
    rank = jnp.dot(bound.astype(f32).astype(bf16), earlier.astype(f32).astype(bf16), preferred_element_type=f32)
    chooser = jnp.where(bound & (rank == (slot % 8).astype(f32)), 1.0, 0.0).astype(bf16)
    rows = jnp.dot(chooser, obs_ref[...], preferred_element_type=f32).reshape(n_lat, 8, d_model)
    live = lax.broadcasted_iota(i32, (8, n_obs), 1) < count_ref[0]
    tags = jnp.where(live, cell_ref[...] + 1, 0).astype(f32).astype(bf16)
    tags = lax.dot_general(tags, chooser, (((1,), (1,)), ((), ())), preferred_element_type=f32)
    at_tag = lax.broadcasted_iota(i32, (n_lat, 8, n_slots), 1) == 6
    send[:, :, :n_slots] = jnp.where(at_tag, tags[None], rows[:, :, :n_slots]).astype(bf16)
    send[:, :, n_slots:] = rows[:, :, n_slots:].astype(bf16)
    recv[lat] = send[lat]

    pl.semaphore_wait(barrier, len(peers))

    def copy(src, dst, sems, k, where):
        return pltpu.make_async_remote_copy(
            src_ref=src, dst_ref=dst, send_sem=sems.at[0, k], recv_sem=sems.at[1, k],
            device_id=where, device_id_type=MESH,
        )

    o_copies = [
        copy(send.at[(lat + k) % n_lat], recv.at[lat], o_sems, k - 1, others[k - 1]) for k in range(1, n_lat)
    ]
    for one in o_copies:
        one.start()
    loads[3].wait()
    n_col, col_rows, _ = own_ref.shape
    lon_dev = tok_ref.shape[0] // col_rows
    margin = n_col - lon_dev
    n_tok = lon_dev * col_rows
    place = lax.broadcasted_iota(i32, (n_tok, n_tok), 0)
    cell = (place % col_rows) * lon_dev + place // col_rows
    mover = jnp.where(cell == lax.broadcasted_iota(i32, (n_tok, n_tok), 1), 1.0, 0.0).astype(bf16)
    turned = jnp.dot(mover, tok_ref[...], preferred_element_type=f32)
    for one in o_copies:
        one.wait_recv()
    got = recv[...].astype(f32)
    slots = got[:, :, :n_slots]
    sub = lax.broadcasted_iota(i32, slots.shape, 1)
    tag = jnp.sum(jnp.where(sub == 6, slots, 0.0), axis=1, keepdims=True)
    lane = lax.broadcasted_iota(i32, slots.shape, 2)
    tag = jnp.sum(jnp.where(lane == lat * 8 + sub, tag, 0.0), axis=2, keepdims=True)
    tag = tag.reshape(n_slots, 1)
    place = lax.broadcasted_iota(i32, (n_slots, n_tok), 1)
    cell = (place % col_rows) * lon_dev + place // col_rows + 1
    placer = jnp.where(tag == cell.astype(f32), 1.0, 0.0).astype(bf16)
    added = lax.dot_general(
        placer, got.reshape(n_slots, d_model).astype(bf16), (((0,), (0,)), ((), ())), preferred_element_type=f32
    )
    own_ref[:lon_dev] = (turned + added).astype(bf16).reshape(lon_dev, col_rows, d_model)

    wide = d_model // 2
    direct = [(j, 0, d_model) for j in range(margin - 2)] + [(margin - 2, 0, wide)]
    around = [(margin - 2, wide, wide), (margin - 1, 0, wide), (margin - 1, wide, wide)]

    def part_of(ref, col, piece):
        return ref.at[col + piece[0], :, pl.ds(piece[1], piece[2])]

    first = [copy(part_of(own_ref, 0, p), r_one.at[i], r_sems.at[0], i, up) for i, p in enumerate(around)]
    second = [copy(r_one.at[i], r_two.at[i], r_sems.at[1], i, up) for i, p in enumerate(around)]
    third = [
        copy(r_two.at[i], part_of(own_ref, lon_dev, p), r_sems.at[2], i, last) for i, p in enumerate(around)
    ]
    e_copies = [
        copy(part_of(own_ref, 0, p), part_of(own_ref, lon_dev, p), e_sems, i, west) for i, p in enumerate(direct)
    ]
    for one in first + e_copies:
        one.start()
    half = lon_dev // 2
    n_copies = [
        copy(own_ref.at[pl.ds(h * half, half)], next_ref.at[pl.ds(h * half, half)], n_sems, h, south)
        for h in range(2)
    ]
    c_copies = [
        copy(part_of(own_ref, lon_dev, p), part_of(next_ref, lon_dev, p), c_sems, i, south)
        for i, p in enumerate(direct + around)
    ]

    @pl.when(lat > 0)
    def _():
        for one in n_copies:
            one.start()

    @pl.when(lat == n_lat - 1)
    def _():
        next_ref[...] = jnp.zeros_like(next_ref)

    for came, onward in zip(first + second, second + third):
        came.wait_recv()
        onward.start()
    for i, one in enumerate(e_copies + third):
        one.wait_recv()

        @pl.when(lat > 0)
        def _():
            c_copies[i].start()

    @pl.when(lat < n_lat - 1)
    def _():
        for one in n_copies + c_copies:
            one.wait_recv()

    @pl.when(lat > 0)
    def _():
        for one in n_copies + c_copies:
            one.wait_send()

    for one in o_copies + e_copies + first + second + third:
        one.wait_send()
    for one in loads[4:]:
        one.wait()


def block_part(
    lat_dev, shift_ref, own_ref, next_ref, gain_ref, w_qkv_ref, w_out_ref, cot_ref, out_ref, g_ref,
    region_ref, qkv_ref, ctx_ref, ctx_t_ref,
):
    n_tok, d_model = region_ref.shape
    n_src = own_ref.shape[0] * own_ref.shape[1]
    lon_dev = 2 * WIN
    col_rows = n_tok // lon_dev
    lat_shift, lon_shift = shift_ref[0, 0], shift_ref[0, 1]
    base = lax.axis_index("lat") * lat_dev + lat_shift
    limit = lax.axis_size("lat") * lat_dev
    token = lax.broadcasted_iota(jnp.int32, (n_tok, n_src), 0)
    row = (token // lon_dev) % lat_dev + lat_shift
    source = (token % lon_dev + lon_shift) * col_rows + (token // (lon_dev * lat_dev)) * lat_dev + row
    source = source - lax.broadcasted_iota(jnp.int32, (n_tok, n_src), 1)
    here = jnp.where((source == 0) & (row < lat_dev), 1.0, 0.0).astype(jnp.bfloat16)
    after = jnp.where((source == lat_dev) & (row >= lat_dev), 1.0, 0.0)
    after = jnp.where(row + lax.axis_index("lat") * lat_dev < limit, after, 0.0).astype(jnp.bfloat16)
    region_ref[...] = jnp.dot(here, own_ref[...].reshape(n_src, d_model), preferred_element_type=jnp.float32) + jnp.dot(
        after, next_ref[...].reshape(n_src, d_model), preferred_element_type=jnp.float32
    )
    head_dim = d_model // HEADS
    pair = 2 * head_dim
    groups = n_tok // (2 * WIN)
    win_tok = n_tok // 2
    as_float = region_ref[...]
    average = jnp.mean(as_float, axis=-1, keepdims=True)
    centred = as_float - average
    variance = jnp.mean(centred * centred, axis=-1, keepdims=True)
    normed = (centred * lax.rsqrt(variance + 1e-05) * gain_ref[...]).astype(jnp.bfloat16)
    block = 512
    for col in range(0, 3 * d_model, block):
        part = jnp.dot(normed, w_qkv_ref[:, col : col + block], preferred_element_type=jnp.float32)
        part = part.reshape(groups, 2, WIN, block)
        for win in range(2):
            qkv_ref[win, :, col : col + block] = part[:, win].reshape(win_tok, block).astype(jnp.bfloat16)
    lane = lax.broadcasted_iota(jnp.int32, (win_tok, pair), 1)
    first = lane < head_dim
    key = lax.broadcasted_iota(jnp.int32, (win_tok, 2 * win_tok), 1)
    is_valid = base + (key // WIN) % WIN < limit
    for win in range(2):
        for two in range(HEADS // 2):
            at = two * pair
            queries = qkv_ref[win, :, at : at + pair]
            keys = qkv_ref[win, :, d_model + at : d_model + at + pair]
            values = qkv_ref[win, :, 2 * d_model + at : 2 * d_model + at + pair]
            zero = jnp.zeros_like(keys)
            keys = jnp.concatenate([jnp.where(first, keys, zero), jnp.where(first, zero, keys)], axis=0)
            values = jnp.concatenate([jnp.where(first, values, zero), jnp.where(first, zero, values)], axis=0)
            scores = lax.dot_general(
                queries, keys, (((1,), (1,)), ((), ())), preferred_element_type=jnp.float32
            ) * head_dim ** (-0.5)
            scores = jnp.where(is_valid, scores, -1e30)
            weights = []
            for half in range(2):
                mine = scores[:, half * win_tok : (half + 1) * win_tok]
                powers = jnp.exp(mine - jnp.max(mine, axis=-1, keepdims=True))
                weights.append((powers / jnp.sum(powers, axis=-1, keepdims=True)).astype(jnp.bfloat16))
            context = jnp.dot(jnp.concatenate(weights, axis=1), values, preferred_element_type=jnp.float32)
            ctx_ref[:, win, :, at : at + pair] = context.reshape(groups, WIN, pair)
    context = ctx_ref[...].reshape(n_tok, d_model).astype(jnp.bfloat16)
    for col in range(0, d_model, block):
        result = jnp.dot(context, w_out_ref[:, col : col + block], preferred_element_type=jnp.float32)
        out_ref[:, col : col + block] = (region_ref[:, col : col + block] + result).astype(jnp.bfloat16)
    ctx_t_ref[...] = context.T
    cores, n_x, n_y, rows, wide = g_ref.shape
    n_z = rows // 16
    for x in range(n_x):
        part = jnp.dot(
            ctx_t_ref[...], cot_ref[:, x * wide : (x + 1) * wide], preferred_element_type=jnp.float32
        ).astype(jnp.bfloat16)
        for z in range(n_z):
            for core in range(cores):
                for y in range(n_y):
                    at = ((z * cores + core) * n_y + y) * 16
                    g_ref[core, x, y, z * 16 : (z + 1) * 16, :] = part[at : at + 16, :]


def reduce_part(
    n_x, n_y, n_h, n_l,
    g_ref, out_ref,
    c_recv_a, c_recv_b, x_send, x_recv, x_sum, y_send, y_recv, y_sum,
    a_send, a_recv, b_send, b_recv, z_own, z_send, z_recv,
    c_sems, x_sems, y_sems, a_sems, b_sems, z_sems,
):
    lon, lat, y = lax.axis_index("lon"), lax.axis_index("lat"), lax.axis_index("dp")
    x, z_hi = lon // n_h, lon % n_h
    z_lo, core = lat // 2, lat % 2
    f32, bf16 = jnp.float32, jnp.bfloat16

    def at_x(k):
        return {"lon": ((x + k) % n_x) * n_h + z_hi}

    def at_y(k):
        return {"dp": (y + k) % n_y}

    pal = {"lat": z_lo * 2 + 1 - core}
    copies = []

    def send(src, dst, sems, k, where):
        one = pltpu.make_async_remote_copy(
            src_ref=src, dst_ref=dst, send_sem=sems.at[0, k], recv_sem=sems.at[1, k],
            device_id=where, device_id_type=MESH,
        )
        one.start()
        copies.append(one)
        return one

    _, _, _, rows, wide = g_ref.shape
    half = rows // 2
    low, high = pl.ds(0, half), pl.ds(half, half)
    order = [2, 1, 3, 0]
    c_a, c_b = {}, {}
    for i, k in enumerate(order):
        dest = (x + k) % n_x
        c_a[k] = send(g_ref.at[1 - core, dest, :, low], c_recv_a.at[k], c_sems, 2 * i, pal)
        dest = (y + k) % n_y
        c_b[k] = send(g_ref.at[1 - core, :, dest, high], c_recv_b.at[k], c_sems, 2 * i + 1, pal)
    x_c, y_c = {}, {}
    for k in order:
        c_a[k].wait_recv()
        dest = (x + k) % n_x
        for i in range(n_y):
            part = g_ref[core, dest, i, :half].astype(f32) + c_recv_a[k, i].astype(f32)
            if k:
                x_send[k - 1, i] = part.astype(bf16)
            else:
                x_sum[i] = part
        if k:
            x_c[k] = send(x_send.at[k - 1], x_recv.at[k - 1], x_sems, k - 1, at_x(k))
        c_b[k].wait_recv()
        dest = (y + k) % n_y
        for i in range(n_x):
            part = g_ref[core, i, dest, half:].astype(f32) + c_recv_b[k, i].astype(f32)
            if k:
                y_send[k - 1, i] = part.astype(bf16)
            else:
                y_sum[i] = part
        if k:
            y_c[k] = send(y_send.at[k - 1], y_recv.at[k - 1], y_sems, k - 1, at_y(k))
    for k in range(1, n_x):
        x_c[k].wait_recv()
    a_c, b_c = {}, {}
    for k in order:
        dest = (y + k) % n_y
        part_a = x_sum[dest]
        for j in range(n_x - 1):
            part_a = part_a + x_recv[j, dest].astype(f32)
        if k:
            a_send[k - 1] = part_a.astype(bf16)
            a_c[k] = send(a_send.at[k - 1], a_recv.at[k - 1], a_sems, k - 1, at_y(k))
    for k in range(1, n_y):
        y_c[k].wait_recv()
    for k in order:
        dest = (x + k) % n_x
        part_b = y_sum[dest]
        for j in range(n_y - 1):
            part_b = part_b + y_recv[j, dest].astype(f32)
        if k:
            b_send[k - 1] = part_b.astype(bf16)
            b_c[k] = send(b_send.at[k - 1], b_recv.at[k - 1], b_sems, k - 1, at_x(k))
    for k in range(1, n_y):
        a_c[k].wait_recv()
        part_a = part_a + a_recv[k - 1].astype(f32)
    for k in range(1, n_x):
        b_c[k].wait_recv()
        part_b = part_b + b_recv[k - 1].astype(f32)
    each = rows // n_l
    span = wide // n_h
    for place, whole in ((0, part_a), (n_l // 2, part_b)):
        for i in range(n_l // 2):
            for j in range(n_h):
                tile = whole[i * each : (i + 1) * each, j * span : (j + 1) * span]
                z_own[place + i, j] = jnp.concatenate([tile[: each // 2], tile[each // 2 :]], axis=1)
    z_send[...] = z_own[...].astype(bf16)
    z_c = []
    for a in (2, 1, 3, 0):
        for b in (4, 3, 5, 2, 6, 1, 7, 0):
            if a or b:
                z_to, l_to = (z_hi + a) % n_h, (z_lo + b) % n_l
                at = {"lon": x * n_h + z_to, "lat": l_to * 2 + core}
                k = a * n_l + b - 1
                z_c.append((k, send(z_send.at[l_to, z_to], z_recv.at[k], z_sems, k, at)))
    part = z_own[z_lo, z_hi]
    for k, one in reversed(z_c):
        one.wait_recv()
        part = part + z_recv[k].astype(f32)
    out_ref[: each // 2] = part[:, :span]
    out_ref[each // 2 :] = part[:, span:]
    for one in copies:
        one.wait_send()


def whole_kernel(lat_dev, n_x, n_y, n_h, n_l, count_ref, shift_ref, *refs):
    loaded, refs = refs[:8], refs[8:]
    (out_ref, grad_ref), refs = refs[:2], refs[2:]
    (own_ref, next_ref), held, refs = refs[:2], refs[2:6], refs[6:]
    moved, refs = refs[:14], refs[14:]
    g_ref, (region_ref, qkv_ref, ctx_ref, ctx_t_ref), refs = refs[0], refs[1:5], refs[5:]
    lon, y = lax.axis_index("lon"), lax.axis_index("dp")
    x, z_hi = lon // n_h, lon % n_h
    peers = [{"lon": ((x + k) % n_x) * n_h + z_hi} for k in range(1, n_x)]
    peers += [{"dp": (y + k) % n_y} for k in range(1, n_y)]
    peers += [{"lon": x * n_h + (z_hi + k) % n_h} for k in (1, n_h - 1)]
    exchange_part(n_x, n_h, peers, count_ref, *loaded, own_ref, next_ref, *held, *moved)
    gain_ref, w_qkv_ref, w_out_ref, cot_ref = held
    block_part(
        lat_dev, shift_ref, own_ref, next_ref, gain_ref, w_qkv_ref, w_out_ref, cot_ref, out_ref, g_ref,
        region_ref, qkv_ref, ctx_ref, ctx_t_ref,
    )
    reduce_part(n_x, n_y, n_h, n_l, g_ref, grad_ref, *refs)


def run_whole(count, shift, arrays, lat_dev, n_lat, n_x, n_y, n_h):
    tokens, obs, lats, cells = arrays[:4]
    n_tok, d_model = tokens.shape
    margin = WIN - 1
    n_col, col_rows = 2 * WIN + margin, n_tok // (2 * WIN)
    n_l = n_lat // 2
    rows, wide = d_model // (2 * n_y), d_model // n_x
    half = rows // 2
    vmem = pl.BlockSpec(memory_space=pltpu.VMEM)
    smem = pl.BlockSpec(memory_space=pltpu.SMEM)
    bf16, f32 = jnp.bfloat16, jnp.float32
    sems = pltpu.SemaphoreType.DMA
    like = [pltpu.VMEM(one.shape, one.dtype) for one in arrays]
    return pl.pallas_call(
        functools.partial(whole_kernel, lat_dev, n_x, n_y, n_h, n_l),
        out_shape=[
            jax.ShapeDtypeStruct((n_tok, d_model), bf16),
            jax.ShapeDtypeStruct((16, wide // n_h), f32),
        ],
        in_specs=[smem, smem] + [pl.BlockSpec(memory_space=pltpu.HBM)] * len(arrays),
        out_specs=[vmem, vmem],
        scratch_shapes=[
            pltpu.VMEM((n_col, col_rows, d_model), bf16),
            pltpu.VMEM((n_col, col_rows, d_model), bf16),
        ]
        + like[4:]
        + like[:4]
        + [
            pltpu.VMEM((n_lat, 8, d_model), bf16),
            pltpu.VMEM((n_lat, 8, d_model), bf16),
            pltpu.VMEM((3, col_rows, d_model // 2), bf16),
            pltpu.VMEM((3, col_rows, d_model // 2), bf16),
            sems((len(arrays),)),
            sems((2, n_lat - 1)),
            sems((2, margin - 1)),
            sems((2, 2)),
            sems((2, margin + 2)),
            sems((3, 2, 3)),
            pltpu.VMEM((2, n_x, n_y, rows, wide), bf16),
            pltpu.VMEM((n_tok, d_model), f32),
            pltpu.VMEM((2, n_tok // 2, 3 * d_model), bf16),
            pltpu.VMEM((n_tok // (2 * WIN), 2, WIN, d_model), f32),
            pltpu.VMEM((d_model, n_tok), bf16),
            pltpu.VMEM((n_x, n_y, half, wide), bf16),
            pltpu.VMEM((n_y, n_x, half, wide), bf16),
            pltpu.VMEM((n_x - 1, n_y, half, wide), bf16),
            pltpu.VMEM((n_x - 1, n_y, half, wide), bf16),
            pltpu.VMEM((n_y, half, wide), f32),
            pltpu.VMEM((n_y - 1, n_x, half, wide), bf16),
            pltpu.VMEM((n_y - 1, n_x, half, wide), bf16),
            pltpu.VMEM((n_x, half, wide), f32),
            pltpu.VMEM((n_y - 1, half, wide), bf16),
            pltpu.VMEM((n_y - 1, half, wide), bf16),
            pltpu.VMEM((n_x - 1, half, wide), bf16),
            pltpu.VMEM((n_x - 1, half, wide), bf16),
            pltpu.VMEM((n_l, n_h, 8, wide // 2), f32),
            pltpu.VMEM((n_l, n_h, 8, wide // 2), bf16),
            pltpu.VMEM((n_l * n_h - 1, 8, wide // 2), bf16),
            sems((2, 2 * n_x)),
            sems((2, n_x - 1)),
            sems((2, n_y - 1)),
            sems((2, n_y - 1)),
            sems((2, n_x - 1)),
            sems((2, n_l * n_h - 1)),
        ],
        compiler_params=pltpu.CompilerParams(
            collective_id=0, has_side_effects=True, vmem_limit_bytes=56 << 20
        ),
        name="whole",
    )(count, shift, *[pltpu.with_memory_space_constraint(one, pltpu.HBM) for one in arrays])


def on_device(
    tokens,
    norm_gain,
    w_qkv,
    w_out,
    obs_vectors,
    obs_lat,
    obs_cell,
    obs_count,
    shift_offsets,
    cotangent,
):
    n_batch, levels, lat_dev, lon_dev, d_model = tokens.shape
    n_lat = lax.axis_size("lat")
    n_dp = lax.axis_size("dp")
    n_hi = 4
    n_x = lax.axis_size("lon") // n_hi
    n_obs = obs_vectors.shape[0]
    arrays = (
        tokens.reshape(-1, d_model),
        obs_vectors,
        obs_lat.reshape(1, n_obs),
        obs_cell[None, :],
        norm_gain[None, :],
        w_qkv,
        w_out,
        cotangent.reshape(-1, d_model),
    )
    mixed, gradient = run_whole(obs_count, shift_offsets, arrays, lat_dev, n_lat, n_x, n_dp, n_hi)
    return (mixed.reshape(tokens.shape), gradient.T)


def solution(mesh):
    placed = (
        P("dp", None, "lat", "lon", None),
        P(),
        P(),
        P(),
        P(("lon", "lat", "dp"), None),
        P(("lon", "lat", "dp"), None),
        P(("lon", "lat", "dp")),
        P(("lon", "lat", "dp")),
        P("dp", None),
        P("dp", None, "lat", "lon", None),
    )
    return jax.shard_map(
        on_device,
        mesh=mesh,
        in_specs=placed,
        out_specs=(P("dp", None, "lat", "lon", None), P("lon", ("lat", "dp"))),
        check_vma=False,
    )
```

```python
import functools

import jax
import jax.numpy as jnp
from jax import lax
from jax.experimental import pallas as pl
from jax.experimental.pallas import tpu as pltpu
from jax.sharding import PartitionSpec as P

HEADS = 16
WIN = 8
MESH = pl.DeviceIdType.MESH


def exchange_part(
    n_x, n_h, peers,
    count_ref, tok_hbm, obs_hbm, lat_hbm, cell_hbm, gain_hbm, w_qkv_hbm, w_out_hbm, cot_hbm,
    own_ref, next_ref, gain_ref, w_qkv_ref, w_out_ref, cot_ref,
    tok_ref, obs_ref, lat_ref, cell_ref, send, recv, r_one, r_two,
    l_sems, o_sems, e_sems, n_sems, c_sems, r_sems, cot_pal_ref, s_sems,
):
    loads = []
    for src, dst in (
        (lat_hbm, lat_ref), (cell_hbm, cell_ref), (obs_hbm, obs_ref), (tok_hbm, tok_ref),
        (gain_hbm, gain_ref), (cot_hbm, cot_ref), (w_qkv_hbm, w_qkv_ref), (w_out_hbm, w_out_ref),
    ):
        loads.append(pltpu.make_async_copy(src, dst, l_sems.at[len(loads)]))
        loads[-1].start()
    lon, lat = lax.axis_index("lon"), lax.axis_index("lat")
    n_lon = n_x * n_h
    n_lat = send.shape[0]
    f32, bf16, i32 = jnp.float32, jnp.bfloat16, jnp.int32
    x, z_hi = lon // n_h, lon % n_h
    west = {"lon": (lon + n_lon - 1) % n_lon}
    east = {"lon": (lon + 1) % n_lon}
    south = {"lat": (lat + n_lat - 1) % n_lat}
    others = [{"lat": (lat + k) % n_lat} for k in range(1, n_lat)]
    up = {"lon": x * n_h + (z_hi + 1) % n_h}
    turn = jnp.where(z_hi == n_h - 2, n_x - 1, 0)
    last = {"lon": ((x + turn) % n_x) * n_h + (z_hi + 1) % n_h}
    turn = jnp.where(z_hi == n_h - 1, 1, 0)
    before = {"lon": ((x + turn) % n_x) * n_h + (z_hi + n_h - 1) % n_h}
    barrier = pltpu.get_barrier_semaphore()
    peers = others + [west, east, last, before] + peers
    for peer in peers:
        pl.semaphore_signal(barrier, inc=1, device_id=peer, device_id_type=MESH)

    for one in loads[:3]:
        one.wait()
    n_obs, d_model = obs_ref.shape
    n_slots = n_lat * 8
    slot = lax.broadcasted_iota(i32, (n_slots, n_obs), 0)
    bound = lat_ref[...] == slot // 8
    earlier = lax.broadcasted_iota(i32, (n_obs, n_obs), 0) < lax.broadcasted_iota(i32, (n_obs, n_obs), 1)
    rank = jnp.dot(bound.astype(f32).astype(bf16), earlier.astype(f32).astype(bf16), preferred_element_type=f32)
    quarter = d_model // 4
    seat = slot % 8

    def chosen(wanted):
        return jnp.where(bound & (rank == wanted.astype(f32)), 1.0, 0.0).astype(bf16)

    chooser = chosen(seat)
    last_part = obs_ref[:, 3 * quarter :]
    live = lax.broadcasted_iota(i32, (8, n_obs), 1) < count_ref[0]
    tags = jnp.where(live, cell_ref[...] + 1, 0).astype(f32).astype(bf16)
    tags = lax.dot_general(tags, chooser, (((1,), (1,)), ((), ())), preferred_element_type=f32)
    at_tag = lax.broadcasted_iota(i32, (n_lat, 8, n_slots), 1) == 6
    send[:, :, 3 * quarter :] = jnp.where(at_tag, tags[None], 0.0).astype(bf16)
    for j in range(3):
        cols = slice(j * quarter, (j + 1) * quarter)
        rows = jnp.dot(chooser, obs_ref[:, cols], preferred_element_type=f32)
        extra = chosen(jnp.where(seat < 6, -1, (seat - 6) * 3 + j))
        rows = rows + jnp.dot(extra, last_part, preferred_element_type=f32)
        send[:, :, cols] = rows.reshape(n_lat, 8, quarter).astype(bf16)
    recv[lat] = send[lat]

    pl.semaphore_wait(barrier, len(peers))

    def copy(src, dst, sems, k, where):
        return pltpu.make_async_remote_copy(
            src_ref=src, dst_ref=dst, send_sem=sems.at[0, k], recv_sem=sems.at[1, k],
            device_id=where, device_id_type=MESH,
        )

    o_copies = [
        copy(send.at[(lat + k) % n_lat], recv.at[lat], o_sems, k - 1, others[k - 1]) for k in range(1, n_lat)
    ]
    for one in o_copies:
        one.start()
    swap = copy(cot_hbm, cot_pal_ref, s_sems, 0, {"lat": lat + 1 - 2 * (lat % 2)})
    swap.start()
    loads[3].wait()
    n_col, col_rows, _ = own_ref.shape
    lon_dev = tok_ref.shape[0] // col_rows
    margin = n_col - lon_dev
    n_tok = lon_dev * col_rows
    place = lax.broadcasted_iota(i32, (n_tok, n_tok), 0)
    cell = (place % col_rows) * lon_dev + place // col_rows
    mover = jnp.where(cell == lax.broadcasted_iota(i32, (n_tok, n_tok), 1), 1.0, 0.0).astype(bf16)
    turned = jnp.dot(mover, tok_ref[...], preferred_element_type=f32)
    for one in o_copies:
        one.wait_recv()
    got = recv[...].astype(f32)
    slots = got[:, :, 3 * quarter :]
    sub = lax.broadcasted_iota(i32, slots.shape, 1)
    tag = jnp.sum(jnp.where(sub == 6, slots, 0.0), axis=1, keepdims=True)
    lane = lax.broadcasted_iota(i32, slots.shape, 2) - lat * 8
    place = lax.broadcasted_iota(i32, (n_slots, n_tok), 1)
    cell = (place % col_rows) * lon_dev + place // col_rows + 1
    got = got.reshape(n_slots, 3 * quarter + n_slots).astype(bf16)

    def placed(wanted, cols):
        mine = jnp.sum(jnp.where(lane == wanted, tag, 0.0), axis=2, keepdims=True).reshape(n_slots, 1)
        placer = jnp.where(mine == cell.astype(f32), 1.0, 0.0).astype(bf16)
        return lax.dot_general(placer, got[:, cols], (((0,), (0,)), ((), ())), preferred_element_type=f32)

    added = [placed(sub, slice(0, 3 * quarter)), 0.0]
    for j in range(3):
        wanted = jnp.where(sub < 6, -1 - lat * 8, (sub - 6) * 3 + j)
        added[1] = added[1] + placed(wanted, slice(j * quarter, (j + 1) * quarter))
    added = jnp.concatenate(added, axis=1)
    own_ref[:lon_dev] = (turned + added).astype(bf16).reshape(lon_dev, col_rows, d_model)

    wide = d_model // 2
    direct = [(j, 0, d_model) for j in range(margin - 2)] + [(margin - 2, 0, wide)]
    around = [(margin - 2, wide, wide), (margin - 1, 0, wide), (margin - 1, wide, wide)]

    def part_of(ref, col, piece):
        return ref.at[col + piece[0], :, pl.ds(piece[1], piece[2])]

    first = [copy(part_of(own_ref, 0, p), r_one.at[i], r_sems.at[0], i, up) for i, p in enumerate(around)]
    second = [copy(r_one.at[i], r_two.at[i], r_sems.at[1], i, up) for i, p in enumerate(around)]
    third = [
        copy(r_two.at[i], part_of(own_ref, lon_dev, p), r_sems.at[2], i, last) for i, p in enumerate(around)
    ]
    e_copies = [
        copy(part_of(own_ref, 0, p), part_of(own_ref, lon_dev, p), e_sems, i, west) for i, p in enumerate(direct)
    ]
    for one in first + e_copies:
        one.start()
    half = lon_dev // 2
    n_copies = [
        copy(own_ref.at[pl.ds(h * half, half)], next_ref.at[pl.ds(h * half, half)], n_sems, h, south)
        for h in range(2)
    ]
    c_copies = [
        copy(part_of(own_ref, lon_dev, p), part_of(next_ref, lon_dev, p), c_sems, i, south)
        for i, p in enumerate(direct + around)
    ]

    @pl.when(lat > 0)
    def _():
        for one in n_copies:
            one.start()

    @pl.when(lat == n_lat - 1)
    def _():
        next_ref[...] = jnp.zeros_like(next_ref)

    for came, onward in zip(first + second, second + third):
        came.wait_recv()
        onward.start()
    for i, one in enumerate(e_copies + third):
        one.wait_recv()

        @pl.when(lat > 0)
        def _():
            c_copies[i].start()

    @pl.when(lat < n_lat - 1)
    def _():
        for one in n_copies + c_copies:
            one.wait_recv()

    @pl.when(lat > 0)
    def _():
        for one in n_copies + c_copies:
            one.wait_send()

    for one in o_copies + e_copies + first + second + third:
        one.wait_send()
    for one in loads[4:]:
        one.wait()
    swap.wait()


def block_part(
    lat_dev, shift_ref, own_ref, next_ref, gain_ref, w_qkv_ref, w_out_ref, out_ref,
    region_ref, qkv_ref, ctx_ref, ctx_t_ref, ctx_pal_ref, s_sems,
):
    n_tok, d_model = region_ref.shape
    n_src = own_ref.shape[0] * own_ref.shape[1]
    lon_dev = 2 * WIN
    col_rows = n_tok // lon_dev
    lat_shift, lon_shift = shift_ref[0, 0], shift_ref[0, 1]
    base = lax.axis_index("lat") * lat_dev + lat_shift
    limit = lax.axis_size("lat") * lat_dev
    token = lax.broadcasted_iota(jnp.int32, (n_tok, n_src), 0)
    row = (token // lon_dev) % lat_dev + lat_shift
    source = (token % lon_dev + lon_shift) * col_rows + (token // (lon_dev * lat_dev)) * lat_dev + row
    source = source - lax.broadcasted_iota(jnp.int32, (n_tok, n_src), 1)
    here = jnp.where((source == 0) & (row < lat_dev), 1.0, 0.0).astype(jnp.bfloat16)
    after = jnp.where((source == lat_dev) & (row >= lat_dev), 1.0, 0.0)
    after = jnp.where(row + lax.axis_index("lat") * lat_dev < limit, after, 0.0).astype(jnp.bfloat16)
    region_ref[...] = jnp.dot(here, own_ref[...].reshape(n_src, d_model), preferred_element_type=jnp.float32) + jnp.dot(
        after, next_ref[...].reshape(n_src, d_model), preferred_element_type=jnp.float32
    )
    head_dim = d_model // HEADS
    pair = 2 * head_dim
    groups = n_tok // (2 * WIN)
    win_tok = n_tok // 2
    as_float = region_ref[...]
    average = jnp.mean(as_float, axis=-1, keepdims=True)
    centred = as_float - average
    variance = jnp.mean(centred * centred, axis=-1, keepdims=True)
    normed = (centred * lax.rsqrt(variance + 1e-05) * gain_ref[...]).astype(jnp.bfloat16)
    block = 512
    for col in range(0, 3 * d_model, block):
        part = jnp.dot(normed, w_qkv_ref[:, col : col + block], preferred_element_type=jnp.float32)
        part = part.reshape(groups, 2, WIN, block)
        for win in range(2):
            qkv_ref[win, :, col : col + block] = part[:, win].reshape(win_tok, block).astype(jnp.bfloat16)
    lane = lax.broadcasted_iota(jnp.int32, (win_tok, pair), 1)
    first = lane < head_dim
    key = lax.broadcasted_iota(jnp.int32, (win_tok, 2 * win_tok), 1)
    is_valid = base + (key // WIN) % WIN < limit
    for win in range(2):
        for two in range(HEADS // 2):
            at = two * pair
            queries = qkv_ref[win, :, at : at + pair]
            keys = qkv_ref[win, :, d_model + at : d_model + at + pair]
            values = qkv_ref[win, :, 2 * d_model + at : 2 * d_model + at + pair]
            zero = jnp.zeros_like(keys)
            keys = jnp.concatenate([jnp.where(first, keys, zero), jnp.where(first, zero, keys)], axis=0)
            values = jnp.concatenate([jnp.where(first, values, zero), jnp.where(first, zero, values)], axis=0)
            scores = lax.dot_general(
                queries, keys, (((1,), (1,)), ((), ())), preferred_element_type=jnp.float32
            ) * head_dim ** (-0.5)
            scores = jnp.where(is_valid, scores, -1e30)
            weights = []
            for half in range(2):
                mine = scores[:, half * win_tok : (half + 1) * win_tok]
                powers = jnp.exp(mine - jnp.max(mine, axis=-1, keepdims=True))
                weights.append((powers / jnp.sum(powers, axis=-1, keepdims=True)).astype(jnp.bfloat16))
            context = jnp.dot(jnp.concatenate(weights, axis=1), values, preferred_element_type=jnp.float32)
            ctx_ref[:, win, :, at : at + pair] = context.reshape(groups, WIN, pair)
    context = ctx_ref[...].reshape(n_tok, d_model).astype(jnp.bfloat16)
    ctx_t_ref[...] = context.T.reshape(ctx_t_ref.shape)
    lat = lax.axis_index("lat")
    swap = pltpu.make_async_remote_copy(
        src_ref=ctx_t_ref.at[:, 1 - lat % 2], dst_ref=ctx_pal_ref, send_sem=s_sems.at[0, 1],
        recv_sem=s_sems.at[1, 1], device_id={"lat": lat + 1 - 2 * (lat % 2)}, device_id_type=MESH,
    )
    swap.start()
    for col in range(0, d_model, block):
        result = jnp.dot(context, w_out_ref[:, col : col + block], preferred_element_type=jnp.float32)
        out_ref[:, col : col + block] = (region_ref[:, col : col + block] + result).astype(jnp.bfloat16)
    swap.wait()


def reduce_part(
    n_x, n_y, n_h, n_l,
    ctx_t_ref, ctx_pal_ref, cot_ref, cot_pal_ref, out_ref,
    x_send, x_recv, x_sum, y_send, y_recv, y_sum, a_send, a_recv, b_send, b_recv, z_own, z_send, z_recv,
    x_sems, y_sems, a_sems, b_sems, z_sems,
):
    lon, lat, y = lax.axis_index("lon"), lax.axis_index("lat"), lax.axis_index("dp")
    x, z_hi = lon // n_h, lon % n_h
    z_lo, core = lat // 2, lat % 2
    f32, bf16 = jnp.float32, jnp.bfloat16

    def at_x(k):
        return {"lon": ((x + k) % n_x) * n_h + z_hi}

    def at_y(k):
        return {"dp": (y + k) % n_y}

    copies = []

    def send(src, dst, sems, k, where):
        one = pltpu.make_async_remote_copy(
            src_ref=src, dst_ref=dst, send_sem=sems.at[0, k], recv_sem=sems.at[1, k],
            device_id=where, device_id_type=MESH,
        )
        one.start()
        copies.append(one)
        return one

    n_tok, d_model = cot_ref.shape
    wide = d_model // n_x
    half = (n_l // 2) * 16
    order = [2, 1, 3, 0]
    mine = ctx_t_ref[:, core].reshape(d_model // 2, n_tok)
    theirs = ctx_pal_ref[...].reshape(d_model // 2, n_tok)
    x_c, y_c = {}, {}
    for k in order:
        dest = (x + k) % n_x
        cols = pl.ds(pl.multiple_of(dest * wide, wide), wide)
        part = jnp.dot(mine, cot_ref[:, cols], preferred_element_type=f32)
        part = part + jnp.dot(theirs, cot_pal_ref[:, cols], preferred_element_type=f32)
        part = part.reshape(n_l, n_y, 16, wide)
        for i in range(n_y):
            low = part[: n_l // 2, i].reshape(half, wide)
            high = part[n_l // 2 :, i].reshape(half, wide)
            if k:
                x_send[k - 1, i] = low.astype(bf16)
            else:
                x_sum[i] = low
            y_sum[i, dest] = high
            y_send[i, dest] = high.astype(bf16)
        if k:
            x_c[k] = send(x_send.at[k - 1], x_recv.at[k - 1], x_sems, k - 1, at_x(k))
    for k in order[:3]:
        y_c[k] = send(y_send.at[(y + k) % n_y], y_recv.at[k - 1], y_sems, k - 1, at_y(k))
    for k in range(1, n_x):
        x_c[k].wait_recv()
    a_c, b_c = {}, {}
    for k in order:
        dest = (y + k) % n_y
        part_a = x_sum[dest]
        for j in range(n_x - 1):
            part_a = part_a + x_recv[j, dest].astype(f32)
        if k:
            a_send[k - 1] = part_a.astype(bf16)
            a_c[k] = send(a_send.at[k - 1], a_recv.at[k - 1], a_sems, k - 1, at_y(k))
    for k in range(1, n_y):
        y_c[k].wait_recv()
    for k in order:
        dest = (x + k) % n_x
        part_b = y_sum[y, dest]
        for j in range(n_y - 1):
            part_b = part_b + y_recv[j, dest].astype(f32)
        if k:
            b_send[k - 1] = part_b.astype(bf16)
            b_c[k] = send(b_send.at[k - 1], b_recv.at[k - 1], b_sems, k - 1, at_x(k))
    for k in range(1, n_y):
        a_c[k].wait_recv()
        part_a = part_a + a_recv[k - 1].astype(f32)
    for k in range(1, n_x):
        b_c[k].wait_recv()
        part_b = part_b + b_recv[k - 1].astype(f32)
    each = 16
    span = wide // n_h
    for place, whole in ((0, part_a), (n_l // 2, part_b)):
        for i in range(n_l // 2):
            for j in range(n_h):
                tile = whole[i * each : (i + 1) * each, j * span : (j + 1) * span]
                z_own[place + i, j] = jnp.concatenate([tile[: each // 2], tile[each // 2 :]], axis=1)
    z_send[...] = z_own[...].astype(bf16)
    z_c = []
    for a in (2, 1, 3, 0):
        for b in (4, 3, 5, 2, 6, 1, 7, 0):
            if a or b:
                z_to, l_to = (z_hi + a) % n_h, (z_lo + b) % n_l
                at = {"lon": x * n_h + z_to, "lat": l_to * 2 + core}
                k = a * n_l + b - 1
                z_c.append((k, send(z_send.at[l_to, z_to], z_recv.at[k], z_sems, k, at)))
    part = z_own[z_lo, z_hi]
    for k, one in reversed(z_c):
        one.wait_recv()
        part = part + z_recv[k].astype(f32)
    out_ref[: each // 2] = part[:, :span]
    out_ref[each // 2 :] = part[:, span:]
    for one in copies:
        one.wait_send()


def whole_kernel(lat_dev, n_x, n_y, n_h, n_l, count_ref, shift_ref, *refs):
    loaded, refs = refs[:8], refs[8:]
    (out_ref, grad_ref), refs = refs[:2], refs[2:]
    (own_ref, next_ref), held, refs = refs[:2], refs[2:6], refs[6:]
    moved, refs = refs[:14], refs[14:]
    (cot_pal_ref, s_sems), refs = refs[:2], refs[2:]
    (region_ref, qkv_ref, ctx_ref, ctx_t_ref, ctx_pal_ref), refs = refs[:5], refs[5:]
    lon, y = lax.axis_index("lon"), lax.axis_index("dp")
    x, z_hi = lon // n_h, lon % n_h
    peers = [{"lon": ((x + k) % n_x) * n_h + z_hi} for k in range(1, n_x)]
    peers += [{"dp": (y + k) % n_y} for k in range(1, n_y)]
    peers += [{"lon": x * n_h + (z_hi + k) % n_h} for k in (1, n_h - 1)]
    exchange_part(n_x, n_h, peers, count_ref, *loaded, own_ref, next_ref, *held, *moved, cot_pal_ref, s_sems)
    gain_ref, w_qkv_ref, w_out_ref, cot_ref = held
    block_part(
        lat_dev, shift_ref, own_ref, next_ref, gain_ref, w_qkv_ref, w_out_ref, out_ref,
        region_ref, qkv_ref, ctx_ref, ctx_t_ref, ctx_pal_ref, s_sems,
    )
    reduce_part(n_x, n_y, n_h, n_l, ctx_t_ref, ctx_pal_ref, cot_ref, cot_pal_ref, grad_ref, *refs)


def run_whole(count, shift, arrays, lat_dev, n_lat, n_x, n_y, n_h):
    tokens, obs, lats, cells = arrays[:4]
    n_tok, d_model = tokens.shape
    margin = WIN - 1
    n_col, col_rows = 2 * WIN + margin, n_tok // (2 * WIN)
    n_l = n_lat // 2
    rows, wide = d_model // (2 * n_y), d_model // n_x
    half = rows // 2
    vmem = pl.BlockSpec(memory_space=pltpu.VMEM)
    smem = pl.BlockSpec(memory_space=pltpu.SMEM)
    bf16, f32 = jnp.bfloat16, jnp.float32
    sems = pltpu.SemaphoreType.DMA
    like = [pltpu.VMEM(one.shape, one.dtype) for one in arrays]
    return pl.pallas_call(
        functools.partial(whole_kernel, lat_dev, n_x, n_y, n_h, n_l),
        out_shape=[
            jax.ShapeDtypeStruct((n_tok, d_model), bf16),
            jax.ShapeDtypeStruct((16, wide // n_h), f32),
        ],
        in_specs=[smem, smem] + [pl.BlockSpec(memory_space=pltpu.HBM)] * len(arrays),
        out_specs=[vmem, vmem],
        scratch_shapes=[
            pltpu.VMEM((n_col, col_rows, d_model), bf16),
            pltpu.VMEM((n_col, col_rows, d_model), bf16),
        ]
        + like[4:]
        + like[:4]
        + [
            pltpu.VMEM((n_lat, 8, d_model - d_model // 4 + n_lat * 8), bf16),
            pltpu.VMEM((n_lat, 8, d_model - d_model // 4 + n_lat * 8), bf16),
            pltpu.VMEM((3, col_rows, d_model // 2), bf16),
            pltpu.VMEM((3, col_rows, d_model // 2), bf16),
            sems((len(arrays),)),
            sems((2, n_lat - 1)),
            sems((2, margin - 1)),
            sems((2, 2)),
            sems((2, margin + 2)),
            sems((3, 2, 3)),
            pltpu.VMEM((n_tok, d_model), bf16),
            sems((2, 2)),
            pltpu.VMEM((n_tok, d_model), f32),
            pltpu.VMEM((2, n_tok // 2, 3 * d_model), bf16),
            pltpu.VMEM((n_tok // (2 * WIN), 2, WIN, d_model), f32),
            pltpu.VMEM((n_l, 2, rows // 2, n_tok), bf16),
            pltpu.VMEM((n_l, rows // 2, n_tok), bf16),
            pltpu.VMEM((n_x - 1, n_y, half, wide), bf16),
            pltpu.VMEM((n_x - 1, n_y, half, wide), bf16),
            pltpu.VMEM((n_y, half, wide), f32),
            pltpu.VMEM((n_y, n_x, half, wide), bf16),
            pltpu.VMEM((n_y - 1, n_x, half, wide), bf16),
            pltpu.VMEM((n_y, n_x, half, wide), f32),
            pltpu.VMEM((n_y - 1, half, wide), bf16),
            pltpu.VMEM((n_y - 1, half, wide), bf16),
            pltpu.VMEM((n_x - 1, half, wide), bf16),
            pltpu.VMEM((n_x - 1, half, wide), bf16),
            pltpu.VMEM((n_l, n_h, 8, wide // 2), f32),
            pltpu.VMEM((n_l, n_h, 8, wide // 2), bf16),
            pltpu.VMEM((n_l * n_h - 1, 8, wide // 2), bf16),
            sems((2, n_x - 1)),
            sems((2, n_y - 1)),
            sems((2, n_y - 1)),
            sems((2, n_x - 1)),
            sems((2, n_l * n_h - 1)),
        ],
        compiler_params=pltpu.CompilerParams(
            collective_id=0, has_side_effects=True, vmem_limit_bytes=40 << 20
        ),
        name="whole",
    )(count, shift, *[pltpu.with_memory_space_constraint(one, pltpu.HBM) for one in arrays])


def on_device(
    tokens,
    norm_gain,
    w_qkv,
    w_out,
    obs_vectors,
    obs_lat,
    obs_cell,
    obs_count,
    shift_offsets,
    cotangent,
):
    n_batch, levels, lat_dev, lon_dev, d_model = tokens.shape
    n_lat = lax.axis_size("lat")
    n_dp = lax.axis_size("dp")
    n_hi = 4
    n_x = lax.axis_size("lon") // n_hi
    n_obs = obs_vectors.shape[0]
    arrays = (
        tokens.reshape(-1, d_model),
        obs_vectors,
        obs_lat.reshape(1, n_obs),
        obs_cell[None, :],
        norm_gain[None, :],
        w_qkv,
        w_out,
        cotangent.reshape(-1, d_model),
    )
    mixed, gradient = run_whole(obs_count, shift_offsets, arrays, lat_dev, n_lat, n_x, n_dp, n_hi)
    return (mixed.reshape(tokens.shape), gradient.T)


def solution(mesh):
    placed = (
        P("dp", None, "lat", "lon", None),
        P(),
        P(),
        P(),
        P(("lon", "lat", "dp"), None),
        P(("lon", "lat", "dp"), None),
        P(("lon", "lat", "dp")),
        P(("lon", "lat", "dp")),
        P("dp", None),
        P("dp", None, "lat", "lon", None),
    )
    return jax.shard_map(
        on_device,
        mesh=mesh,
        in_specs=placed,
        out_specs=(P("dp", None, "lat", "lon", None), P("lon", ("lat", "dp"))),
        check_vma=False,
    )
```

```python
import functools

import jax
import jax.numpy as jnp
from jax import lax
from jax.experimental import pallas as pl
from jax.experimental.pallas import tpu as pltpu
from jax.sharding import PartitionSpec as P

HEADS = 16
WIN = 8
MESH = pl.DeviceIdType.MESH


def exchange_part(
    n_x, n_h, peers,
    count_ref, tok_hbm, obs_hbm, lat_hbm, cell_hbm, gain_hbm, w_qkv_hbm, w_out_hbm, cot_hbm,
    own_ref, next_ref, gain_ref, w_qkv_ref, w_out_ref, cot_ref,
    tok_ref, obs_ref, lat_ref, cell_ref, send, recv, r_one, r_two,
    l_sems, o_sems, e_sems, n_sems, c_sems, r_sems, cot_pal_ref, s_sems,
):
    loads = []
    for src, dst in (
        (lat_hbm, lat_ref), (cell_hbm, cell_ref), (obs_hbm, obs_ref), (tok_hbm, tok_ref),
        (gain_hbm, gain_ref), (cot_hbm, cot_ref), (w_qkv_hbm, w_qkv_ref), (w_out_hbm, w_out_ref),
    ):
        loads.append(pltpu.make_async_copy(src, dst, l_sems.at[len(loads)]))
        loads[-1].start()
    lon, lat = lax.axis_index("lon"), lax.axis_index("lat")
    n_lon = n_x * n_h
    n_lat = send.shape[0]
    f32, bf16, i32 = jnp.float32, jnp.bfloat16, jnp.int32
    x, z_hi = lon // n_h, lon % n_h
    west = {"lon": (lon + n_lon - 1) % n_lon}
    east = {"lon": (lon + 1) % n_lon}
    south = {"lat": (lat + n_lat - 1) % n_lat}
    others = [{"lat": (lat + k) % n_lat} for k in range(1, n_lat)]
    up = {"lon": x * n_h + (z_hi + 1) % n_h}
    turn = jnp.where(z_hi == n_h - 2, n_x - 1, 0)
    last = {"lon": ((x + turn) % n_x) * n_h + (z_hi + 1) % n_h}
    turn = jnp.where(z_hi == n_h - 1, 1, 0)
    before = {"lon": ((x + turn) % n_x) * n_h + (z_hi + n_h - 1) % n_h}
    barrier = pltpu.get_barrier_semaphore()
    peers = others + [west, east, last, before] + peers
    for peer in peers:
        pl.semaphore_signal(barrier, inc=1, device_id=peer, device_id_type=MESH)

    for one in loads[:3]:
        one.wait()
    n_obs, d_model = obs_ref.shape
    n_slots = n_lat * 8
    slot = lax.broadcasted_iota(i32, (n_slots, n_obs), 0)
    bound = lat_ref[...] == slot // 8
    earlier = lax.broadcasted_iota(i32, (n_obs, n_obs), 0) < lax.broadcasted_iota(i32, (n_obs, n_obs), 1)
    rank = jnp.dot(bound.astype(f32).astype(bf16), earlier.astype(f32).astype(bf16), preferred_element_type=f32)
    quarter = d_model // 4
    seat = slot % 8

    def chosen(wanted):
        return jnp.where(bound & (rank == wanted.astype(f32)), 1.0, 0.0).astype(bf16)

    chooser = chosen(seat)
    last_part = obs_ref[:, 3 * quarter :]
    live = lax.broadcasted_iota(i32, (8, n_obs), 1) < count_ref[0]
    tags = jnp.where(live, cell_ref[...] + 1, 0).astype(f32).astype(bf16)
    tags = lax.dot_general(tags, chooser, (((1,), (1,)), ((), ())), preferred_element_type=f32)
    at_tag = lax.broadcasted_iota(i32, (n_lat, 8, n_slots), 1) == 6
    send[:, :, 3 * quarter :] = jnp.where(at_tag, tags[None], 0.0).astype(bf16)
    for j in range(3):
        cols = slice(j * quarter, (j + 1) * quarter)
        rows = jnp.dot(chooser, obs_ref[:, cols], preferred_element_type=f32)
        extra = chosen(jnp.where(seat < 6, -1, (seat - 6) * 3 + j))
        rows = rows + jnp.dot(extra, last_part, preferred_element_type=f32)
        send[:, :, cols] = rows.reshape(n_lat, 8, quarter).astype(bf16)
    recv[lat] = send[lat]

    pl.semaphore_wait(barrier, len(peers))

    def copy(src, dst, sems, k, where):
        return pltpu.make_async_remote_copy(
            src_ref=src, dst_ref=dst, send_sem=sems.at[0, k], recv_sem=sems.at[1, k],
            device_id=where, device_id_type=MESH,
        )

    o_copies = [
        copy(send.at[(lat + k) % n_lat], recv.at[lat], o_sems, k - 1, others[k - 1]) for k in range(1, n_lat)
    ]
    for one in o_copies:
        one.start()
    swap = copy(cot_hbm, cot_pal_ref, s_sems, 0, {"lat": lat + 1 - 2 * (lat % 2)})
    swap.start()
    loads[3].wait()
    n_col, col_rows, _ = own_ref.shape
    lon_dev = tok_ref.shape[0] // col_rows
    margin = n_col - lon_dev
    n_tok = lon_dev * col_rows
    place = lax.broadcasted_iota(i32, (n_tok, n_tok), 0)
    cell = (place % col_rows) * lon_dev + place // col_rows
    mover = jnp.where(cell == lax.broadcasted_iota(i32, (n_tok, n_tok), 1), 1.0, 0.0).astype(bf16)
    turned = jnp.dot(mover, tok_ref[...], preferred_element_type=f32)
    for one in o_copies:
        one.wait_recv()
    got = recv[...].astype(f32)
    slots = got[:, :, 3 * quarter :]
    sub = lax.broadcasted_iota(i32, slots.shape, 1)
    tag = jnp.sum(jnp.where(sub == 6, slots, 0.0), axis=1, keepdims=True)
    lane = lax.broadcasted_iota(i32, slots.shape, 2) - lat * 8
    place = lax.broadcasted_iota(i32, (n_slots, n_tok), 1)
    cell = (place % col_rows) * lon_dev + place // col_rows + 1
    got = got.reshape(n_slots, 3 * quarter + n_slots).astype(bf16)

    def placed(wanted, cols):
        mine = jnp.sum(jnp.where(lane == wanted, tag, 0.0), axis=2, keepdims=True).reshape(n_slots, 1)
        placer = jnp.where(mine == cell.astype(f32), 1.0, 0.0).astype(bf16)
        return lax.dot_general(placer, got[:, cols], (((0,), (0,)), ((), ())), preferred_element_type=f32)

    added = [placed(sub, slice(0, 3 * quarter)), 0.0]
    for j in range(3):
        wanted = jnp.where(sub < 6, -1 - lat * 8, (sub - 6) * 3 + j)
        added[1] = added[1] + placed(wanted, slice(j * quarter, (j + 1) * quarter))
    added = jnp.concatenate(added, axis=1)
    own_ref[:lon_dev] = (turned + added).astype(bf16).reshape(lon_dev, col_rows, d_model)

    wide = d_model // 2
    direct = [(j, 0, d_model) for j in range(margin - 2)] + [(margin - 2, 0, wide)]
    piece_w = d_model // 4
    around = [(margin - 2, c * piece_w, piece_w) for c in (2, 3)]
    around += [(margin - 1, c * piece_w, piece_w) for c in range(4)]

    def part_of(ref, col, piece):
        return ref.at[col + piece[0], :, pl.ds(piece[1], piece[2])]

    first = [copy(part_of(own_ref, 0, p), r_one.at[i], r_sems.at[0], i, up) for i, p in enumerate(around)]
    second = [copy(r_one.at[i], r_two.at[i], r_sems.at[1], i, up) for i, p in enumerate(around)]
    third = [
        copy(r_two.at[i], part_of(own_ref, lon_dev, p), r_sems.at[2], i, last) for i, p in enumerate(around)
    ]
    e_copies = [
        copy(part_of(own_ref, 0, p), part_of(own_ref, lon_dev, p), e_sems, i, west) for i, p in enumerate(direct)
    ]
    for one in first + e_copies:
        one.start()
    half = lon_dev // 2
    n_copies = [
        copy(own_ref.at[pl.ds(h * half, half)], next_ref.at[pl.ds(h * half, half)], n_sems, h, south)
        for h in range(2)
    ]
    c_copies = [
        copy(part_of(own_ref, lon_dev, p), part_of(next_ref, lon_dev, p), c_sems, i, south)
        for i, p in enumerate(direct + around)
    ]

    @pl.when(lat > 0)
    def _():
        for one in n_copies:
            one.start()

    @pl.when(lat == n_lat - 1)
    def _():
        next_ref[...] = jnp.zeros_like(next_ref)

    for came, onward in zip(first + second, second + third):
        came.wait_recv()
        onward.start()
    for i, one in enumerate(e_copies + third):
        one.wait_recv()

        @pl.when(lat > 0)
        def _():
            c_copies[i].start()

    @pl.when(lat < n_lat - 1)
    def _():
        for one in n_copies + c_copies:
            one.wait_recv()

    @pl.when(lat > 0)
    def _():
        for one in n_copies + c_copies:
            one.wait_send()

    for one in o_copies + e_copies + first + second + third:
        one.wait_send()
    for one in loads[4:]:
        one.wait()
    swap.wait()


def block_part(
    lat_dev, shift_ref, own_ref, next_ref, gain_ref, w_qkv_ref, w_out_ref, out_ref,
    region_ref, qkv_ref, ctx_ref, ctx_t_ref, ctx_pal_ref, s_sems,
):
    n_tok, d_model = region_ref.shape
    n_src = own_ref.shape[0] * own_ref.shape[1]
    lon_dev = 2 * WIN
    col_rows = n_tok // lon_dev
    lat_shift, lon_shift = shift_ref[0, 0], shift_ref[0, 1]
    base = lax.axis_index("lat") * lat_dev + lat_shift
    limit = lax.axis_size("lat") * lat_dev
    token = lax.broadcasted_iota(jnp.int32, (n_tok, n_src), 0)
    row = (token // lon_dev) % lat_dev + lat_shift
    source = (token % lon_dev + lon_shift) * col_rows + (token // (lon_dev * lat_dev)) * lat_dev + row
    source = source - lax.broadcasted_iota(jnp.int32, (n_tok, n_src), 1)
    here = jnp.where((source == 0) & (row < lat_dev), 1.0, 0.0).astype(jnp.bfloat16)
    after = jnp.where((source == lat_dev) & (row >= lat_dev), 1.0, 0.0)
    after = jnp.where(row + lax.axis_index("lat") * lat_dev < limit, after, 0.0).astype(jnp.bfloat16)
    region_ref[...] = jnp.dot(here, own_ref[...].reshape(n_src, d_model), preferred_element_type=jnp.float32) + jnp.dot(
        after, next_ref[...].reshape(n_src, d_model), preferred_element_type=jnp.float32
    )
    head_dim = d_model // HEADS
    pair = 2 * head_dim
    groups = n_tok // (2 * WIN)
    win_tok = n_tok // 2
    as_float = region_ref[...]
    average = jnp.mean(as_float, axis=-1, keepdims=True)
    centred = as_float - average
    variance = jnp.mean(centred * centred, axis=-1, keepdims=True)
    normed = (centred * lax.rsqrt(variance + 1e-05) * gain_ref[...]).astype(jnp.bfloat16)
    block = 512
    for col in range(0, 3 * d_model, block):
        part = jnp.dot(normed, w_qkv_ref[:, col : col + block], preferred_element_type=jnp.float32)
        part = part.reshape(groups, 2, WIN, block)
        for win in range(2):
            qkv_ref[win, :, col : col + block] = part[:, win].reshape(win_tok, block).astype(jnp.bfloat16)
    lane = lax.broadcasted_iota(jnp.int32, (win_tok, pair), 1)
    first = lane < head_dim
    key = lax.broadcasted_iota(jnp.int32, (win_tok, 2 * win_tok), 1)
    is_valid = base + (key // WIN) % WIN < limit
    for win in range(2):
        for two in range(HEADS // 2):
            at = two * pair
            queries = qkv_ref[win, :, at : at + pair]
            keys = qkv_ref[win, :, d_model + at : d_model + at + pair]
            values = qkv_ref[win, :, 2 * d_model + at : 2 * d_model + at + pair]
            zero = jnp.zeros_like(keys)
            keys = jnp.concatenate([jnp.where(first, keys, zero), jnp.where(first, zero, keys)], axis=0)
            values = jnp.concatenate([jnp.where(first, values, zero), jnp.where(first, zero, values)], axis=0)
            scores = lax.dot_general(
                queries, keys, (((1,), (1,)), ((), ())), preferred_element_type=jnp.float32
            ) * head_dim ** (-0.5)
            scores = jnp.where(is_valid, scores, -1e30)
            weights = []
            for half in range(2):
                mine = scores[:, half * win_tok : (half + 1) * win_tok]
                powers = jnp.exp(mine - jnp.max(mine, axis=-1, keepdims=True))
                weights.append((powers / jnp.sum(powers, axis=-1, keepdims=True)).astype(jnp.bfloat16))
            context = jnp.dot(jnp.concatenate(weights, axis=1), values, preferred_element_type=jnp.float32)
            ctx_ref[:, win, :, at : at + pair] = context.reshape(groups, WIN, pair)
    context = ctx_ref[...].reshape(n_tok, d_model).astype(jnp.bfloat16)
    ctx_t_ref[...] = context.T.reshape(ctx_t_ref.shape)
    lat = lax.axis_index("lat")
    swap = pltpu.make_async_remote_copy(
        src_ref=ctx_t_ref.at[:, 1 - lat % 2], dst_ref=ctx_pal_ref, send_sem=s_sems.at[0, 1],
        recv_sem=s_sems.at[1, 1], device_id={"lat": lat + 1 - 2 * (lat % 2)}, device_id_type=MESH,
    )
    swap.start()
    for col in range(0, d_model, block):
        result = jnp.dot(context, w_out_ref[:, col : col + block], preferred_element_type=jnp.float32)
        out_ref[:, col : col + block] = (region_ref[:, col : col + block] + result).astype(jnp.bfloat16)
    swap.wait()


def reduce_part(
    n_x, n_y, n_h, n_l,
    ctx_t_ref, ctx_pal_ref, cot_ref, cot_pal_ref, out_ref,
    x_send, x_recv, x_sum, y_send, y_recv, y_sum, a_send, a_recv, b_send, b_recv, z_own, z_send, z_recv,
    x_sems, y_sems, a_sems, b_sems, z_sems,
):
    lon, lat, y = lax.axis_index("lon"), lax.axis_index("lat"), lax.axis_index("dp")
    x, z_hi = lon // n_h, lon % n_h
    z_lo, core = lat // 2, lat % 2
    f32, bf16 = jnp.float32, jnp.bfloat16

    def at_x(k):
        return {"lon": ((x + k) % n_x) * n_h + z_hi}

    def at_y(k):
        return {"dp": (y + k) % n_y}

    copies = []

    def send(src, dst, sems, k, where):
        one = pltpu.make_async_remote_copy(
            src_ref=src, dst_ref=dst, send_sem=sems.at[0, k], recv_sem=sems.at[1, k],
            device_id=where, device_id_type=MESH,
        )
        one.start()
        copies.append(one)
        return one

    n_tok, d_model = cot_ref.shape
    wide = d_model // n_x
    half = (n_l // 2) * 16
    order = [2, 1, 3, 0]
    mine = ctx_t_ref[:, core].reshape(d_model // 2, n_tok)
    theirs = ctx_pal_ref[...].reshape(d_model // 2, n_tok)
    x_c, y_c = {}, {}
    for k in order:
        dest = (x + k) % n_x
        cols = pl.ds(pl.multiple_of(dest * wide, wide), wide)
        part = jnp.dot(mine, cot_ref[:, cols], preferred_element_type=f32)
        part = part + jnp.dot(theirs, cot_pal_ref[:, cols], preferred_element_type=f32)
        part = part.reshape(n_l, n_y, 16, wide)
        for i in range(n_y):
            low = part[: n_l // 2, i].reshape(half, wide)
            high = part[n_l // 2 :, i].reshape(half, wide)
            if k:
                x_send[k - 1, i] = low.astype(bf16)
            else:
                x_sum[i] = low
            y_sum[i, dest] = high
            y_send[i, dest] = high.astype(bf16)
        if k:
            x_c[k] = send(x_send.at[k - 1], x_recv.at[k - 1], x_sems, k - 1, at_x(k))
    for k in order[:3]:
        y_c[k] = send(y_send.at[(y + k) % n_y], y_recv.at[k - 1], y_sems, k - 1, at_y(k))
    for k in range(1, n_x):
        x_c[k].wait_recv()
    a_c, b_c = {}, {}
    for k in order:
        dest = (y + k) % n_y
        part_a = x_sum[dest]
        for j in range(n_x - 1):
            part_a = part_a + x_recv[j, dest].astype(f32)
        if k:
            a_send[k - 1] = part_a.astype(bf16)
            a_c[k] = send(a_send.at[k - 1], a_recv.at[k - 1], a_sems, k - 1, at_y(k))
    for k in range(1, n_y):
        y_c[k].wait_recv()
    for k in order:
        dest = (x + k) % n_x
        part_b = y_sum[y, dest]
        for j in range(n_y - 1):
            part_b = part_b + y_recv[j, dest].astype(f32)
        if k:
            b_send[k - 1] = part_b.astype(bf16)
            b_c[k] = send(b_send.at[k - 1], b_recv.at[k - 1], b_sems, k - 1, at_x(k))
    for k in range(1, n_y):
        a_c[k].wait_recv()
        part_a = part_a + a_recv[k - 1].astype(f32)
    for k in range(1, n_x):
        b_c[k].wait_recv()
        part_b = part_b + b_recv[k - 1].astype(f32)
    each = 16
    span = wide // n_h
    for place, whole in ((0, part_a), (n_l // 2, part_b)):
        for i in range(n_l // 2):
            for j in range(n_h):
                tile = whole[i * each : (i + 1) * each, j * span : (j + 1) * span]
                z_own[place + i, j] = jnp.concatenate([tile[: each // 2], tile[each // 2 :]], axis=1)
    z_send[...] = z_own[...].astype(bf16)
    z_c = []
    for a in (2, 1, 3, 0):
        for b in (4, 3, 5, 2, 6, 1, 7, 0):
            if a or b:
                z_to, l_to = (z_hi + a) % n_h, (z_lo + b) % n_l
                at = {"lon": x * n_h + z_to, "lat": l_to * 2 + core}
                k = a * n_l + b - 1
                z_c.append((k, send(z_send.at[l_to, z_to], z_recv.at[k], z_sems, k, at)))
    part = z_own[z_lo, z_hi]
    for k, one in reversed(z_c):
        one.wait_recv()
        part = part + z_recv[k].astype(f32)
    out_ref[: each // 2] = part[:, :span]
    out_ref[each // 2 :] = part[:, span:]
    for one in copies:
        one.wait_send()


def whole_kernel(lat_dev, n_x, n_y, n_h, n_l, count_ref, shift_ref, *refs):
    loaded, refs = refs[:8], refs[8:]
    (out_ref, grad_ref), refs = refs[:2], refs[2:]
    (own_ref, next_ref), held, refs = refs[:2], refs[2:6], refs[6:]
    moved, refs = refs[:14], refs[14:]
    (cot_pal_ref, s_sems), refs = refs[:2], refs[2:]
    (region_ref, qkv_ref, ctx_ref, ctx_t_ref, ctx_pal_ref), refs = refs[:5], refs[5:]
    lon, y = lax.axis_index("lon"), lax.axis_index("dp")
    x, z_hi = lon // n_h, lon % n_h
    peers = [{"lon": ((x + k) % n_x) * n_h + z_hi} for k in range(1, n_x)]
    peers += [{"dp": (y + k) % n_y} for k in range(1, n_y)]
    peers += [{"lon": x * n_h + (z_hi + k) % n_h} for k in (1, n_h - 1)]
    exchange_part(n_x, n_h, peers, count_ref, *loaded, own_ref, next_ref, *held, *moved, cot_pal_ref, s_sems)
    gain_ref, w_qkv_ref, w_out_ref, cot_ref = held
    block_part(
        lat_dev, shift_ref, own_ref, next_ref, gain_ref, w_qkv_ref, w_out_ref, out_ref,
        region_ref, qkv_ref, ctx_ref, ctx_t_ref, ctx_pal_ref, s_sems,
    )
    reduce_part(n_x, n_y, n_h, n_l, ctx_t_ref, ctx_pal_ref, cot_ref, cot_pal_ref, grad_ref, *refs)


def run_whole(count, shift, arrays, lat_dev, n_lat, n_x, n_y, n_h):
    tokens, obs, lats, cells = arrays[:4]
    n_tok, d_model = tokens.shape
    margin = WIN - 1
    n_col, col_rows = 2 * WIN + margin, n_tok // (2 * WIN)
    n_l = n_lat // 2
    rows, wide = d_model // (2 * n_y), d_model // n_x
    half = rows // 2
    vmem = pl.BlockSpec(memory_space=pltpu.VMEM)
    smem = pl.BlockSpec(memory_space=pltpu.SMEM)
    bf16, f32 = jnp.bfloat16, jnp.float32
    sems = pltpu.SemaphoreType.DMA
    like = [pltpu.VMEM(one.shape, one.dtype) for one in arrays]
    return pl.pallas_call(
        functools.partial(whole_kernel, lat_dev, n_x, n_y, n_h, n_l),
        out_shape=[
            jax.ShapeDtypeStruct((n_tok, d_model), bf16),
            jax.ShapeDtypeStruct((16, wide // n_h), f32),
        ],
        in_specs=[smem, smem] + [pl.BlockSpec(memory_space=pltpu.HBM)] * len(arrays),
        out_specs=[vmem, vmem],
        scratch_shapes=[
            pltpu.VMEM((n_col, col_rows, d_model), bf16),
            pltpu.VMEM((n_col, col_rows, d_model), bf16),
        ]
        + like[4:]
        + like[:4]
        + [
            pltpu.VMEM((n_lat, 8, d_model - d_model // 4 + n_lat * 8), bf16),
            pltpu.VMEM((n_lat, 8, d_model - d_model // 4 + n_lat * 8), bf16),
            pltpu.VMEM((6, col_rows, d_model // 4), bf16),
            pltpu.VMEM((6, col_rows, d_model // 4), bf16),
            sems((len(arrays),)),
            sems((2, n_lat - 1)),
            sems((2, margin - 1)),
            sems((2, 2)),
            sems((2, margin + 5)),
            sems((3, 2, 6)),
            pltpu.VMEM((n_tok, d_model), bf16),
            sems((2, 2)),
            pltpu.VMEM((n_tok, d_model), f32),
            pltpu.VMEM((2, n_tok // 2, 3 * d_model), bf16),
            pltpu.VMEM((n_tok // (2 * WIN), 2, WIN, d_model), f32),
            pltpu.VMEM((n_l, 2, rows // 2, n_tok), bf16),
            pltpu.VMEM((n_l, rows // 2, n_tok), bf16),
            pltpu.VMEM((n_x - 1, n_y, half, wide), bf16),
            pltpu.VMEM((n_x - 1, n_y, half, wide), bf16),
            pltpu.VMEM((n_y, half, wide), f32),
            pltpu.VMEM((n_y, n_x, half, wide), bf16),
            pltpu.VMEM((n_y - 1, n_x, half, wide), bf16),
            pltpu.VMEM((n_y, n_x, half, wide), f32),
            pltpu.VMEM((n_y - 1, half, wide), bf16),
            pltpu.VMEM((n_y - 1, half, wide), bf16),
            pltpu.VMEM((n_x - 1, half, wide), bf16),
            pltpu.VMEM((n_x - 1, half, wide), bf16),
            pltpu.VMEM((n_l, n_h, 8, wide // 2), f32),
            pltpu.VMEM((n_l, n_h, 8, wide // 2), bf16),
            pltpu.VMEM((n_l * n_h - 1, 8, wide // 2), bf16),
            sems((2, n_x - 1)),
            sems((2, n_y - 1)),
            sems((2, n_y - 1)),
            sems((2, n_x - 1)),
            sems((2, n_l * n_h - 1)),
        ],
        compiler_params=pltpu.CompilerParams(
            collective_id=0, has_side_effects=True, vmem_limit_bytes=40 << 20
        ),
        name="whole",
    )(count, shift, *[pltpu.with_memory_space_constraint(one, pltpu.HBM) for one in arrays])


def on_device(
    tokens,
    norm_gain,
    w_qkv,
    w_out,
    obs_vectors,
    obs_lat,
    obs_cell,
    obs_count,
    shift_offsets,
    cotangent,
):
    n_batch, levels, lat_dev, lon_dev, d_model = tokens.shape
    n_lat = lax.axis_size("lat")
    n_dp = lax.axis_size("dp")
    n_hi = 4
    n_x = lax.axis_size("lon") // n_hi
    n_obs = obs_vectors.shape[0]
    arrays = (
        tokens.reshape(-1, d_model),
        obs_vectors,
        obs_lat.reshape(1, n_obs),
        obs_cell[None, :],
        norm_gain[None, :],
        w_qkv,
        w_out,
        cotangent.reshape(-1, d_model),
    )
    mixed, gradient = run_whole(obs_count, shift_offsets, arrays, lat_dev, n_lat, n_x, n_dp, n_hi)
    return (mixed.reshape(tokens.shape), gradient.T)


def solution(mesh):
    placed = (
        P("dp", None, "lat", "lon", None),
        P(),
        P(),
        P(),
        P(("lon", "lat", "dp"), None),
        P(("lon", "lat", "dp"), None),
        P(("lon", "lat", "dp")),
        P(("lon", "lat", "dp")),
        P("dp", None),
        P("dp", None, "lat", "lon", None),
    )
    return jax.shard_map(
        on_device,
        mesh=mesh,
        in_specs=placed,
        out_specs=(P("dp", None, "lat", "lon", None), P("lon", ("lat", "dp"))),
        check_vma=False,
    )
```
